256 devices in a mesh: dp: 64 (over z, y, core), mp: 4 (over x).
Axes of the slice: x: 4, y: 4, z: 8, core: 2. Of those that a mesh axis runs over, the one named last changes fastest.
Arguments:
- prefix_hidden: bfloat16 [256, 1024, 2048], P(('dp', 'mp')), may hold values from -6 to 6
- prefix_len: int32 [256], P('dp'), may hold values from 256 to 1024
- actions: float32 [256, 50, 32], P('dp'), may hold values from -6 to 6
- noise: float32 [256, 50, 32], P('dp'), may hold values from -6 to 6
- time_index: int32 [256], P('dp'), may hold values from 0 to 999
- prefix_gain: float32 [2048], replicated, may hold values from 0.25 to 1.75
- key_weight: bfloat16 [2048, 256], P('dp'), may hold values from -0.125 to 0.125
- value_weight: bfloat16 [2048, 256], P('dp'), may hold values from -0.125 to 0.125
- action_in: bfloat16 [32, 1024], replicated, may hold values from -1 to 1
- attn_gain: float32 [1024], replicated, may hold values from 0.25 to 1.75
- query_w: bfloat16 [1024, 2048], P('dp', 'mp'), may hold values from -0.1875 to 0.1875
- akey_w: bfloat16 [1024, 256], P('dp'), may hold values from -0.1875 to 0.1875
- avalue_w: bfloat16 [1024, 256], P('dp'), may hold values from -0.1875 to 0.1875
- out_w: bfloat16 [2048, 1024], P('mp', 'dp'), may hold values from -0.125 to 0.125
- mlp_gain: float32 [1024], replicated, may hold values from 0.25 to 1.75
- gate_w: bfloat16 [1024, 4096], P('dp', 'mp'), may hold values from -0.1875 to 0.1875
- up_w: bfloat16 [1024, 4096], P('dp', 'mp'), may hold values from -0.1875 to 0.1875
- down_w: bfloat16 [4096, 1024], P('mp', 'dp'), may hold values from -0.09375 to 0.09375
- final_gain: float32 [1024], replicated, may hold values from 0.25 to 1.75
- head_w: bfloat16 [1024, 32], replicated, may hold values from -0.1875 to 0.1875
Outputs:
- velocity: float32 [256, 50, 32], P(('dp', 'mp'))
- ep_loss: float32 [256], P(('dp', 'mp'))
The draws below stay inside these ranges and needn't reach their ends.
Inputs may be any that keep to these rules, and one draw needn't show every extreme that they name: `prefix_len`: prefix positions at or above an episode's length are padding that no output reads.
All inputs are finite; a program needn't handle non-finite values.
Results may differ from the reference program's by a relative error of at most 0.009.
Values may be sent and summed in bfloat16 or wider, within the bound.
A program may use at most 64 MiB of HBM per device.

```python
import math
import jax
import jax.numpy as jnp
from jax import lax

D = 2048
DE = 1024
HEADS = 8
HD = 256
FFE = 4096
ADIM = 32
SPAN = 50
PMAX = 1024
TSTEPS = 1000
EPIS = 256


def set_ends(drawn, rng, least, high):
    place = [jax.random.randint(jax.random.fold_in(rng, axis), (), 0, length) for axis, length in enumerate(drawn.shape)]
    widest = drawn.shape.index(max(drawn.shape))
    neighbour = place[:widest] + [(place[widest] + 1) % drawn.shape[widest]] + place[widest + 1:]
    return drawn.at[tuple(place)].set(least).at[tuple(neighbour)].set(high)


def block_levels(own_key, dims, pieces, smallest, top_value):
    factor_of, own = 1.0, jax.random.fold_in(own_key, 6)
    for position, shards_of in pieces:
        heights = jnp.exp(jax.random.uniform(jax.random.fold_in(own, position), (shards_of,), jnp.float32, smallest / len(pieces), top_value / len(pieces)))
        factor_of = factor_of * jnp.repeat(heights, dims[position] // shards_of).reshape([-1 if axis == position else 1 for axis in range(len(dims))])
    return factor_of


def normal_values(own_key, dims, deviation, bound, split=(), kind=jnp.bfloat16):
    drawn = jax.random.normal(own_key, dims, jnp.float32) * deviation
    if len(split) > 0:
        drawn = block_levels(own_key, dims, split, -0.22, 0.18) * drawn
    return jnp.clip(drawn, min=-bound, max=bound).astype(kind)


def setup_inputs(seed: int = 0) -> dict:
    key_of = jax.random.split(jax.random.key(seed), 21)
    prefix_hidden = normal_values(key_of[0], (EPIS, PMAX, D), 1.0, 6.0, ((0, 256),))
    prefix_len = set_ends(jax.random.randint(key_of[1], (EPIS,), PMAX // 4, PMAX + 1), jax.random.fold_in(key_of[1], 1), PMAX // 4, PMAX).astype(jnp.int32)
    actions = normal_values(key_of[2], (EPIS, SPAN, ADIM), 1.0, 6.0, ((0, 64),), jnp.float32)
    noise = normal_values(key_of[3], (EPIS, SPAN, ADIM), 1.0, 6.0, ((0, 64),), jnp.float32)
    time_index = set_ends(jax.random.randint(key_of[4], (EPIS,), 0, TSTEPS), jax.random.fold_in(key_of[4], 1), 0, TSTEPS - 1).astype(jnp.int32)
    prefix_gain = jnp.clip(1.0 + 0.15 * jax.random.normal(key_of[5], (D,), jnp.float32), 0.25, 1.75)
    key_weight = normal_values(key_of[6], (D, HD), D ** -0.5, 0.125, ((0, 64),))
    value_weight = normal_values(key_of[7], (D, HD), D ** -0.5, 0.125, ((0, 64),))
    action_in = normal_values(key_of[8], (ADIM, DE), ADIM ** -0.5, 1.0)
    attn_gain = jnp.clip(1.0 + 0.15 * jax.random.normal(key_of[9], (DE,), jnp.float32), 0.25, 1.75)
    query_w = normal_values(key_of[10], (DE, HEADS * HD), DE ** -0.5, 0.1875, ((0, 64), (1, 4)))
    akey_w = normal_values(key_of[11], (DE, HD), DE ** -0.5, 0.1875, ((0, 64),))
    avalue_w = normal_values(key_of[12], (DE, HD), DE ** -0.5, 0.1875, ((0, 64),))
    out_w = normal_values(key_of[13], (HEADS * HD, DE), (HEADS * HD) ** -0.5, 0.125, ((0, 4), (1, 64)))
    mlp_gain = jnp.clip(1.0 + 0.15 * jax.random.normal(key_of[14], (DE,), jnp.float32), 0.25, 1.75)
    gate_w = normal_values(key_of[15], (DE, FFE), DE ** -0.5, 0.1875, ((0, 64), (1, 4)))
    up_w = normal_values(key_of[16], (DE, FFE), DE ** -0.5, 0.1875, ((0, 64), (1, 4)))
    down_w = normal_values(key_of[17], (FFE, DE), FFE ** -0.5, 0.09375, ((0, 4), (1, 64)))
    final_gain = jnp.clip(1.0 + 0.15 * jax.random.normal(key_of[18], (DE,), jnp.float32), 0.25, 1.75)
    head_w = normal_values(key_of[19], (DE, ADIM), DE ** -0.5, 0.1875)
    return dict(prefix_hidden=prefix_hidden, prefix_len=prefix_len, actions=actions, noise=noise, time_index=time_index, prefix_gain=prefix_gain, key_weight=key_weight, value_weight=value_weight, action_in=action_in, attn_gain=attn_gain, query_w=query_w, akey_w=akey_w, avalue_w=avalue_w, out_w=out_w, mlp_gain=mlp_gain, gate_w=gate_w, up_w=up_w, down_w=down_w, final_gain=final_gain, head_w=head_w)


def rms(values, gain):
    return values * lax.rsqrt(lax.optimization_barrier(jnp.mean(values * values, axis=-1, keepdims=True)) + 1e-06) * gain

def time_embed(times, width):
    half = width // 2
    steps = jnp.arange(half, dtype=jnp.float32)
    period = 0.004 * jnp.power(jnp.float32(1000.0), steps / (half - 1))
    angle = times[:, None] * (2.0 * math.pi) / period[None, :]
    return jnp.concatenate([jnp.sin(angle), jnp.cos(angle)], axis=-1)

def reference(prefix_hidden, prefix_len, actions, noise, time_index, prefix_gain, key_weight, value_weight, action_in, attn_gain, query_w, akey_w, avalue_w, out_w, mlp_gain, gate_w, up_w, down_w, final_gain, head_w):
    times = (time_index.astype(jnp.float32) + 0.5) / TSTEPS
    x_t = times[:, None, None] * noise + (1.0 - times)[:, None, None] * actions
    target = noise - actions
    x_in = x_t.reshape(EPIS * SPAN, ADIM).astype(jnp.bfloat16)
    temb = time_embed(times, DE)
    h0 = jnp.dot(x_in, action_in, preferred_element_type=jnp.float32).reshape(EPIS, SPAN, DE) + temb[:, None, :]
    h0 = h0.reshape(EPIS * SPAN, DE)

    def project(hidden):
        normed = rms(hidden.astype(jnp.float32), prefix_gain).astype(jnp.bfloat16)
        keys = jnp.dot(normed, key_weight, preferred_element_type=jnp.float32).astype(jnp.bfloat16)
        vals = jnp.dot(normed, value_weight, preferred_element_type=jnp.float32).astype(jnp.bfloat16)
        return (keys, vals)
    prefix_keys, prefix_vals = lax.map(project, prefix_hidden)
    normed = rms(h0, attn_gain).astype(jnp.bfloat16)
    query = (jnp.dot(normed, query_w, preferred_element_type=jnp.float32) * HD ** (-0.5)).astype(jnp.bfloat16)
    query = query.reshape(EPIS, SPAN * HEADS, HD)
    akeys = jnp.dot(normed, akey_w, preferred_element_type=jnp.float32).astype(jnp.bfloat16).reshape(EPIS, SPAN, HD)
    avals = jnp.dot(normed, avalue_w, preferred_element_type=jnp.float32).astype(jnp.bfloat16).reshape(EPIS, SPAN, HD)

    def attend(items):
        rows, pkeys, pvals, keys_a, vals_a, length = items
        keys = jnp.concatenate([pkeys, keys_a], axis=0)
        vals = jnp.concatenate([pvals, vals_a], axis=0)
        live = jnp.concatenate([jnp.arange(PMAX, dtype=jnp.int32) < length, jnp.ones((SPAN,), dtype=bool)])
        scores = jnp.dot(rows, keys.T, preferred_element_type=jnp.float32)
        probs = jnp.where(live[None, :], jnp.exp(scores), 0.0)
        total = lax.optimization_barrier(jnp.sum(probs, axis=-1, keepdims=True))
        weighted = jnp.dot(probs.astype(jnp.bfloat16), vals, preferred_element_type=jnp.float32)
        return (weighted / total).astype(jnp.bfloat16)
    attn = lax.map(attend, (query, prefix_keys, prefix_vals, akeys, avals, prefix_len))
    attn = attn.reshape(EPIS * SPAN, HEADS * HD)
    h1 = h0 + jnp.dot(attn, out_w, preferred_element_type=jnp.float32)
    mixed = rms(h1, mlp_gain).astype(jnp.bfloat16)
    gate = jnp.dot(mixed, gate_w, preferred_element_type=jnp.float32)
    upper = jnp.dot(mixed, up_w, preferred_element_type=jnp.float32)
    hidden = (jax.nn.gelu(gate, approximate=True) * upper).astype(jnp.bfloat16)
    h2 = h1 + jnp.dot(hidden, down_w, preferred_element_type=jnp.float32)
    final = rms(h2, final_gain).astype(jnp.bfloat16)
    velocity = jnp.dot(final, head_w, preferred_element_type=jnp.float32).reshape(EPIS, SPAN, ADIM)
    diff = velocity - target
    ep_loss = lax.optimization_barrier(jnp.mean(diff * diff, axis=(1, 2)))
    return (velocity, ep_loss)
```

```python
import functools
import math

import jax
import jax.numpy as jnp
from jax import lax
from jax.experimental import pallas as pl
from jax.experimental.pallas import tpu as pltpu
from jax.sharding import Mesh
from jax.sharding import PartitionSpec as P

TSTEPS = 1000
NZ, NY, NC, NX = 8, 4, 2, 4
DP_MP = ("z", "y", "c", "mp")
DP = ("z", "y", "c")
MESH = pl.DeviceIdType.MESH


class Gather:
    def __init__(self, buf, order, send_sem, recv_sem, where):
        self.buf, self.order = buf, order
        self.ss, self.rs = send_sem, recv_sem
        self.z, self.y, self.c = where
        self.n = 0
        self.sent = []
        self.waiting = []
        self.steps = self.plan()

    def at(self, dim, ring_index, part=None):
        size = NZ if dim == "z" else NY
        ring_index = lax.rem(ring_index + size, size)
        first = dim == self.order[0]
        cols = self.buf.shape[-1]
        if dim == "z":
            if first:
                if part is None:
                    return self.buf.at[ring_index, self.y, self.c]
                return self.buf.at[ring_index, self.y, self.c, :, pl.ds(part * cols // 2, cols // 2)]
            if part is None:
                return self.buf.at[ring_index, :, self.c]
            return self.buf.at[ring_index, pl.ds(part * (NY // 2), NY // 2), self.c]
        if first:
            if part is None:
                return self.buf.at[self.z, ring_index, self.c]
            return self.buf.at[self.z, ring_index, self.c, :, pl.ds(part * cols // 2, cols // 2)]
        if part is None:
            return self.buf.at[:, ring_index, self.c]
        return self.buf.at[pl.ds(part * (NZ // 2), NZ // 2), ring_index, self.c]

    def send(self, view, device):
        k = self.n
        self.n += 1
        copy = pltpu.make_async_remote_copy(
            src_ref=view,
            dst_ref=view,
            send_sem=self.ss.at[k],
            recv_sem=self.rs.at[k],
            device_id=device,
            device_id_type=MESH,
        )
        copy.start()
        self.sent.append(copy)
        self.waiting.append(copy)

    def arrive(self):
        for copy in self.waiting:
            copy.wait_recv()
        self.waiting = []

    def ring_step(self, dim, hop):
        size, me = (NZ, self.z) if dim == "z" else (NY, self.y)
        up = {dim: lax.rem(me + 1, size)}
        down = {dim: lax.rem(me + size - 1, size)}
        self.arrive()
        if hop < size // 2:
            self.send(self.at(dim, me - hop + 1), up)
            self.send(self.at(dim, me + hop - 1), down)
        else:
            self.send(self.at(dim, me - hop + 1, 0), up)
            self.send(self.at(dim, me + hop - 1, 1), down)

    def core_step(self):
        self.arrive()
        self.send(self.buf.at[:, :, self.c], {"c": 1 - self.c})

    def plan(self):
        steps = []
        for dim in self.order:
            for hop in range(1, (NZ if dim == "z" else NY) // 2 + 1):
                steps.append(functools.partial(self.ring_step, dim, hop))
        steps.append(self.core_step)
        steps.append(self.arrive)
        return steps

    def finish(self):
        for copy in self.sent:
            copy.wait_send()


SENDS = 13
ORDERS = ("zy", "yz", "zy", "yz", "yz", "zy", "yz", "zy")
STARTS = (0, 0, 1, 1, 2, 3, 3, 4)


def gather_kernel(*refs):
    n = len(ORDERS)
    blocks, bufs = refs[:n], refs[n : 2 * n]
    send_sem, recv_sem = refs[2 * n :]
    z, y, c = (lax.axis_index(a) for a in ("z", "y", "c"))
    barrier = pltpu.get_barrier_semaphore()
    near = (
        {"z": lax.rem(z + 1, NZ)},
        {"z": lax.rem(z + NZ - 1, NZ)},
        {"y": lax.rem(y + 1, NY)},
        {"y": lax.rem(y + NY - 1, NY)},
        {"c": 1 - c},
    )
    for device in near:
        pl.semaphore_signal(barrier, inc=1, device_id=device, device_id_type=MESH)
    for block, buf in zip(blocks, bufs):
        buf[z, y, c] = block[...]
    pl.semaphore_wait(barrier, len(near))
    gathers = [
        Gather(buf, order, send_sem.at[i], recv_sem.at[i], (z, y, c))
        for i, (buf, order) in enumerate(zip(bufs, ORDERS))
    ]
    last = max(s + len(g.steps) for s, g in zip(STARTS, gathers))
    for tick in range(last):
        for start, g in zip(STARTS, gathers):
            if 0 <= tick - start < len(g.steps):
                g.steps[tick - start]()
    for g in gathers:
        g.finish()


def gather_all(*blocks):
    n = len(blocks)
    vmem = pl.BlockSpec(memory_space=pltpu.VMEM)
    return pl.pallas_call(
        gather_kernel,
        out_shape=[jax.ShapeDtypeStruct((NZ, NY, NC, *b.shape), b.dtype) for b in blocks],
        in_specs=[vmem] * n,
        out_specs=[vmem] * n,
        scratch_shapes=[
            pltpu.SemaphoreType.DMA((n, SENDS)),
            pltpu.SemaphoreType.DMA((n, SENDS)),
        ],
        compiler_params=pltpu.CompilerParams(
            collective_id=0, has_side_effects=True, vmem_limit_bytes=40 << 20
        ),
    )(*blocks)


def from_everyone(value, axis):
    size = lax.axis_size(axis)
    return lax.all_to_all(
        jnp.broadcast_to(value[None], (size, *value.shape)), axis, 0, 0, tiled=True
    )


def sent_and_summed(value, axis):
    size = lax.axis_size(axis)
    parts = value.reshape(size, -1, *value.shape[1:])
    arrived = lax.all_to_all(parts, axis, split_axis=0, concat_axis=0, tiled=True)
    return arrived.astype(jnp.float32).sum(axis=0)


def rms(values, gain):
    return values * lax.rsqrt(jnp.mean(values * values, axis=-1, keepdims=True) + 1e-06) * gain


def time_embed(times, width):
    half = width // 2
    steps = jnp.arange(half, dtype=jnp.float32)
    period = 0.004 * jnp.power(jnp.float32(1000.0), steps / (half - 1))
    angle = times[:, None] * (2.0 * math.pi) / period[None, :]
    return jnp.concatenate([jnp.sin(angle), jnp.cos(angle)], axis=-1)


def attend(query, pkeys, pvals, akeys, avals, lengths):
    live = jnp.arange(pkeys.shape[1], dtype=jnp.int32)[None, :] < lengths[:, None]
    scores = jnp.einsum("erd,epd->erp", query, pkeys, preferred_element_type=jnp.float32)
    probs = jnp.where(live[:, None, :], jnp.exp(scores), 0.0)
    action_scores = jnp.einsum("erd,ecd->erc", query, akeys, preferred_element_type=jnp.float32)
    action_probs = jnp.exp(action_scores)
    denom = jnp.sum(probs, axis=-1) + jnp.sum(action_probs, axis=-1)
    weighted = jnp.einsum(
        "erp,epd->erd", probs.astype(jnp.bfloat16), pvals, preferred_element_type=jnp.float32
    )
    weighted = weighted + jnp.einsum(
        "erc,ecd->erd", action_probs.astype(jnp.bfloat16), avals, preferred_element_type=jnp.float32
    )
    return (weighted / denom[:, :, None]).astype(jnp.bfloat16)


def on_device(
    prefix_hidden,
    prefix_len,
    actions,
    noise,
    time_index,
    prefix_gain,
    key_weight,
    value_weight,
    action_in,
    attn_gain,
    query_w,
    akey_w,
    avalue_w,
    out_w,
    mlp_gain,
    gate_w,
    up_w,
    down_w,
    final_gain,
    head_w,
):
    f32, bf16 = jnp.float32, jnp.bfloat16
    own_eps, positions, width = prefix_hidden.shape
    group_eps, span, adim = actions.shape
    expert = action_in.shape[1]
    head_size = key_weight.shape[1]
    local_heads = query_w.shape[1] // head_size
    rows_total = group_eps * span
    own_rows = own_eps * span
    member = lax.axis_index("mp")
    first_row = member * own_rows
    first_ep = member * own_eps
    blocks = (
        key_weight,
        value_weight,
        query_w,
        jnp.concatenate([akey_w, avalue_w], axis=1),
        out_w.T,
        gate_w,
        up_w,
        down_w.T,
    )
    full = [w.reshape(-1, w.shape[-1]) for w in gather_all(*blocks)]
    key_full, value_full, query_full, action_kv, out_t, gate_full, up_full, down_t = full
    times = (time_index.astype(f32) + 0.5) / TSTEPS
    x_t = times[:, None, None] * noise + (1.0 - times)[:, None, None] * actions
    target = noise - actions
    x_in = x_t.reshape(rows_total, adim).astype(bf16)
    temb = time_embed(times, expert)
    h0 = (
        jnp.dot(x_in, action_in, preferred_element_type=f32).reshape(group_eps, span, expert)
        + temb[:, None, :]
    )
    h0 = h0.reshape(rows_total, expert)
    prefix_normed = rms(
        prefix_hidden.reshape(own_eps * positions, width).astype(f32), prefix_gain
    ).astype(bf16)
    pkeys = (
        jnp.dot(prefix_normed, key_full, preferred_element_type=f32)
        .astype(bf16)
        .reshape(own_eps, positions, head_size)
    )
    pvals = (
        jnp.dot(prefix_normed, value_full, preferred_element_type=f32)
        .astype(bf16)
        .reshape(own_eps, positions, head_size)
    )
    normed = rms(h0, attn_gain).astype(bf16)
    query = (
        jnp.dot(normed, query_full, preferred_element_type=f32) * head_size ** (-0.5)
    ).astype(bf16)
    both = jnp.dot(normed, action_kv, preferred_element_type=f32).astype(bf16)
    akeys = both[:, :head_size].reshape(group_eps, span, head_size)
    avals = both[:, head_size:].reshape(group_eps, span, head_size)
    own_akeys = lax.dynamic_slice_in_dim(akeys, first_ep, own_eps, 0)
    own_avals = lax.dynamic_slice_in_dim(avals, first_ep, own_eps, 0)
    own_lengths = lax.dynamic_slice_in_dim(prefix_len, first_ep, own_eps, 0)
    query_heads = query.reshape(group_eps, span, local_heads, head_size)
    arrived = lax.all_to_all(query_heads, "mp", split_axis=0, concat_axis=2, tiled=True)
    count = arrived.shape[1]
    all_heads = arrived.shape[2]
    flat = arrived.reshape(own_eps, count * all_heads, head_size)
    result = attend(flat, pkeys, pvals, own_akeys, own_avals, own_lengths)
    result = result.reshape(own_eps, count, all_heads, head_size)
    attn = lax.all_to_all(result, "mp", split_axis=2, concat_axis=0, tiled=True)
    attn = attn.reshape(rows_total, local_heads * head_size)
    h0_own = lax.dynamic_slice_in_dim(h0, first_row, own_rows, 0)
    h1 = h0_own + sent_and_summed(
        jnp.einsum("rk,nk->rn", attn, out_t, preferred_element_type=f32).astype(bf16), "mp"
    )
    mixed_own = rms(h1, mlp_gain).astype(bf16)
    mixed = from_everyone(mixed_own, "mp").reshape(rows_total, expert)
    gate = jnp.dot(mixed, gate_full, preferred_element_type=f32)
    upper = jnp.dot(mixed, up_full, preferred_element_type=f32)
    hidden = (jax.nn.gelu(gate, approximate=True) * upper).astype(bf16)
    h2 = h1 + sent_and_summed(
        jnp.einsum("rk,nk->rn", hidden, down_t, preferred_element_type=f32).astype(bf16), "mp"
    )
    final = rms(h2, final_gain).astype(bf16)
    velocity = jnp.dot(final, head_w, preferred_element_type=f32).reshape(own_eps, span, adim)
    own_target = lax.dynamic_slice_in_dim(target, first_ep, own_eps, 0)
    diff = velocity - own_target
    ep_loss = jnp.mean(diff * diff, axis=(1, 2))
    return (velocity, ep_loss)


def solution(mesh):
    split = Mesh(mesh.devices.reshape(NZ, NY, NC, NX), DP_MP)
    placed = (
        P(DP_MP, None, None),
        P(DP),
        P(DP, None, None),
        P(DP, None, None),
        P(DP),
        P(),
        P(DP, None),
        P(DP, None),
        P(),
        P(),
        P(DP, "mp"),
        P(DP, None),
        P(DP, None),
        P("mp", DP),
        P(),
        P(DP, "mp"),
        P(DP, "mp"),
        P("mp", DP),
        P(),
        P(),
    )
    return jax.shard_map(
        on_device,
        mesh=split,
        in_specs=placed,
        out_specs=(P(DP_MP, None, None), P(DP_MP)),
        check_vma=False,
    )
```

```python
import functools
import math

import jax
import jax.numpy as jnp
import numpy as np
from jax import lax
from jax.experimental import pallas as pl
from jax.experimental.pallas import tpu as pltpu
from jax.sharding import Mesh
from jax.sharding import PartitionSpec as P

TSTEPS = 1000
NZ, NY, NC, NX = 8, 4, 2, 4
SIZE = {"z": NZ, "y": NY, "c": NC, "mp": NX}
DP_MP = ("z", "y", "c", "mp")
DP = ("z", "y", "c")
MESH = pl.DeviceIdType.MESH
PAD = 64
SENDS = 160
LOCALS = 32
f32, bf16 = jnp.float32, jnp.bfloat16


def nt(a, b):
    return lax.dot_general(a, b, (((1,), (1,)), ((), ())), preferred_element_type=f32)


def dot(a, b):
    return jnp.dot(a, b, preferred_element_type=f32)


class Link:
    def __init__(self, send_sem, recv_sem):
        self.ss, self.rs = send_sem, recv_sem
        self.me = {a: lax.axis_index(a) for a in SIZE}
        self.sent = []

    def peer(self, axis, step):
        return {axis: lax.rem(self.me[axis] + step + SIZE[axis], SIZE[axis])}

    def send(self, src, dst, axis, step):
        k = len(self.sent)
        copy = pltpu.make_async_remote_copy(
            src_ref=src,
            dst_ref=dst,
            send_sem=self.ss.at[k],
            recv_sem=self.rs.at[k],
            device_id=self.peer(axis, step),
            device_id_type=MESH,
        )
        copy.start()
        self.sent.append(copy)
        return copy


class Gather:
    def __init__(self, link, buf, plan):
        self.link, self.buf = link, buf
        self.waiting = []
        self.steps = []
        for first, (dim, form) in zip((True, False), plan):
            if form == "ring":
                for hop in range(1, SIZE[dim] // 2 + 1):
                    self.steps.append(functools.partial(self.ring, dim, first, hop))
            elif form == "direct":
                self.steps.append(functools.partial(self.direct, dim, first))
            else:
                self.steps.append(functools.partial(self.two, dim, first, 1))
                self.steps.append(functools.partial(self.two, dim, first, 2))
        self.steps.append(self.core)
        self.steps.append(self.arrive)

    def at(self, dim, first, step, part=None):
        me = self.link.me
        i = lax.rem(me[dim] + step + SIZE[dim], SIZE[dim])
        cols = self.buf.shape[-1]
        half = pl.ds(0 if part is None else part * (cols // 2), cols // 2)
        if dim == "z":
            if first:
                if part is None:
                    return self.buf.at[i, me["y"], me["c"]]
                return self.buf.at[i, me["y"], me["c"], :, half]
            if part is None:
                return self.buf.at[i, :, me["c"]]
            return self.buf.at[i, pl.ds(part * (NY // 2), NY // 2), me["c"]]
        if first:
            if part is None:
                return self.buf.at[me["z"], i, me["c"]]
            return self.buf.at[me["z"], i, me["c"], :, half]
        if part is None:
            return self.buf.at[:, i, me["c"]]
        return self.buf.at[pl.ds(part * (NZ // 2), NZ // 2), i, me["c"]]

    def send(self, view, axis, step):
        self.waiting.append(self.link.send(view, view, axis, step))

    def arrive(self):
        for copy in self.waiting:
            copy.wait_recv()
        self.waiting = []

    def ring(self, dim, first, hop):
        self.arrive()
        last = hop == SIZE[dim] // 2
        self.send(self.at(dim, first, 1 - hop, 0 if last else None), dim, 1)
        self.send(self.at(dim, first, hop - 1, 1 if last else None), dim, -1)

    def direct(self, dim, first):
        self.arrive()
        for step in range(1, SIZE[dim]):
            self.send(self.at(dim, first, 0), dim, step)

    def two(self, dim, first, hop):
        self.arrive()
        if hop == 1:
            for step in (1, -1, 2, -2):
                self.send(self.at(dim, first, 0), dim, step)
        else:
            self.send(self.at(dim, first, -2), dim, 1)
            self.send(self.at(dim, first, 2), dim, -1)
            self.send(self.at(dim, first, -2, 0), dim, 2)
            self.send(self.at(dim, first, 2, 1), dim, -2)

    def core(self):
        self.arrive()
        self.send(self.buf.at[:, :, self.link.me["c"]], "c", 1)

    def step(self):
        if self.steps:
            self.steps.pop(0)()

    def finish(self):
        while self.steps:
            self.step()


def flat(ref):
    return ref[...].reshape(-1, ref.shape[-1])


def norm_rows(src, dst, gain, rows, block=16, unroll=4):
    start, count = rows

    def body(i, _):
        at = pl.ds(pl.multiple_of(start + i * block, block), block)
        v = src[at, :].astype(f32)
        scale = lax.rsqrt(jnp.mean(v * v, axis=-1, keepdims=True) + 1e-06)
        dst[at, :] = (v * scale * gain[...]).astype(bf16)
        return 0

    lax.fori_loop(0, count // block, body, 0, unroll=unroll)


def kernel(
    lens,
    tix,
    x_in,
    acts,
    noise,
    prefix,
    inv_period,
    prefix_gain,
    attn_gain,
    mlp_gain,
    final_gain,
    action_in,
    head_t,
    key_w,
    value_w,
    query_w,
    akey_w,
    avalue_w,
    out_t,
    gate_w,
    up_w,
    down_t,
    vel_ref,
    loss_ref,
    kb,
    vb,
    qb,
    ab,
    ob,
    gb,
    ub,
    db,
    pre,
    pk,
    pv,
    ain,
    hdt,
    actv,
    noisev,
    h0,
    an,
    akv,
    qs,
    qall,
    ares,
    aall,
    part,
    r1,
    r2,
    h1,
    mn,
    hid,
    fn,
    send_sem,
    recv_sem,
    local_sem,
):
    link = Link(send_sem, recv_sem)
    me = link.me
    z, y, c, x = (me[a] for a in DP_MP)
    span = 50

    locals_ = []

    def fetch(src, dst):
        copy = pltpu.make_async_copy(src, dst, local_sem.at[len(locals_)])
        copy.start()
        locals_.append(copy)
        return copy

    barrier = pltpu.get_barrier_semaphore()
    near = [("z", s) for s in (1, -1, 2, -2)] + [("y", s) for s in (1, 2, 3)]
    near += [("c", 1)] + [("mp", s) for s in (1, 2, 3)]
    for axis, step in near:
        pl.semaphore_signal(barrier, inc=1, device_id=link.peer(axis, step), device_id_type=MESH)
    early = [
        fetch(key_w, kb.at[z, y, c]),
        fetch(query_w, qb.at[z, y, c]),
        fetch(value_w, vb.at[z, y, c]),
        fetch(akey_w, ab.at[z, y, c, :, pl.ds(0, 256)]),
        fetch(avalue_w, ab.at[z, y, c, :, pl.ds(256, 256)]),
    ]
    small = [
        fetch(action_in, ain),
        fetch(head_t, hdt),
        fetch(acts, actv),
        fetch(noise, noisev),
    ]
    quarter = prefix.shape[0] // 4
    chunks = [
        fetch(prefix.at[pl.ds(i * quarter, quarter)], pre.at[pl.ds(i * quarter, quarter)])
        for i in range(4)
    ]
    late = [
        fetch(out_t, ob.at[z, y, c]),
        fetch(gate_w, gb.at[z, y, c]),
        fetch(up_w, ub.at[z, y, c]),
        fetch(down_t, db.at[z, y, c]),
    ]
    keys = Gather(link, kb, (("z", "two"), ("y", "direct")))
    query = Gather(link, qb, (("z", "two"), ("y", "direct")))
    values = Gather(link, vb, (("y", "direct"), ("z", "two")))
    action = Gather(link, ab, (("z", "two"), ("y", "direct")))
    out = Gather(link, ob, (("y", "ring"), ("z", "ring")))
    gate = Gather(link, gb, (("z", "two"), ("y", "ring")))
    up = Gather(link, ub, (("y", "ring"), ("z", "ring")))
    down = Gather(link, db, (("z", "two"), ("y", "ring")))

    def advance(*gathers):
        for g in gathers:
            g.step()

    for copy in early:
        copy.wait()
    pl.semaphore_wait(barrier, len(near))
    advance(query, keys, values, action)

    for copy in small:
        copy.wait()
    for e in range(4):
        t = (tix[e].astype(f32) + 0.5) * (1.0 / TSTEPS)
        u = t * inv_period[...]
        turn = (u - jnp.floor(u + 0.5)) * (2.0 * math.pi)
        half = turn.shape[1]
        at = pl.ds(e * PAD, PAD)
        mixed = dot(x_in[at, :], ain[...])
        h0[at, 0:half] = mixed[:, 0:half] + jnp.sin(turn)
        h0[at, half:] = mixed[:, half:] + jnp.cos(turn)
    norm_rows(h0, an, attn_gain, (0, 4 * PAD))
    advance(query, keys, values, action)
    for copy in late:
        copy.wait()
    chunks[0].wait()
    norm_rows(pre, pre, prefix_gain, (0, quarter))
    advance(query, keys, values, action)
    advance(gate, out, up)
    chunks[1].wait()
    norm_rows(pre, pre, prefix_gain, (quarter, quarter))
    advance(query, keys, action, values)
    advance(down, out, up, gate)
    chunks[2].wait()
    norm_rows(pre, pre, prefix_gain, (2 * quarter, quarter))
    query.finish()
    q = (dot(an[...], flat(qb)) * 0.0625).astype(bf16)
    for e in range(4):
        for h in range(2):
            qs[e, h] = q[e * PAD : (e + 1) * PAD, h * 256 : (h + 1) * 256]
    queries = [None]
    for step in range(1, NX):
        queries.append(link.send(qs.at[lax.rem(x + step, NX)], qall.at[x], "mp", step))
    qall[x] = qs[x]
    advance(down, out, up, gate)
    chunks[3].wait()
    norm_rows(pre, pre, prefix_gain, (3 * quarter, quarter))
    keys.finish()
    full_key = flat(kb)
    for i in range(4):
        at = pl.ds(i * quarter, quarter)
        pk[at, :] = dot(pre[at, :], full_key).astype(bf16)
    action.finish()
    own = pl.ds(pl.multiple_of(x * PAD, PAD), PAD)
    akv[...] = dot(an[own, :], flat(ab)).astype(bf16)
    advance(down, out, up, gate)
    values.finish()
    full_value = flat(vb)
    for i in range(4):
        at = pl.ds(i * quarter, quarter)
        pv[at, :] = dot(pre[at, :], full_value).astype(bf16)
    advance(down, out, up, gate)

    length = lens[x]
    heads = []
    for step in (0, 1, 2, 3):
        src = lax.rem(x - step + NX, NX)
        if step:
            queries[step].wait_recv()
        rows = qall[src].reshape(2 * PAD, 256)
        s = nt(rows, pk[...])
        live = lax.broadcasted_iota(jnp.int32, s.shape, 1) < length
        p = jnp.where(live, jnp.exp(s), 0.0)
        sa = nt(rows, akv[:, 0:256])
        real = lax.broadcasted_iota(jnp.int32, sa.shape, 1) < span
        pa = jnp.where(real, jnp.exp(sa), 0.0)
        total = jnp.sum(p, axis=-1, keepdims=True) + jnp.sum(pa, axis=-1, keepdims=True)
        mixed = dot(p.astype(bf16), pv[...]) + dot(pa.astype(bf16), akv[:, 256:512])
        done = (mixed / total).astype(bf16).reshape(2, PAD, 256)
        if step:
            ares[step] = done
            heads.append(link.send(ares.at[step], aall.at[x], "mp", -step))
        else:
            aall[x] = done
        advance(down, out, up, gate)

    def exchange(src, dst):
        return [
            link.send(src.at[lax.rem(x + step, NX)], dst.at[step], "mp", step)
            for step in range(1, NX)
        ]

    out.finish()
    for copy in heads:
        copy.wait_recv()
    a0 = aall[:, 0].reshape(4 * PAD, 256)
    a1 = aall[:, 1].reshape(4 * PAD, 256)
    full_out = flat(ob)
    for j in range(4):
        w = full_out[j * 256 : (j + 1) * 256]
        value = (nt(a0, w[:, 0:256]) + nt(a1, w[:, 256:512])).astype(bf16)
        part[:, :, j * 256 : (j + 1) * 256] = value.reshape(4, PAD, 256)
    sums = exchange(part, r1)
    advance(down, up, gate)
    own_h0 = h0[own, :] + part[x].astype(f32)
    for copy in sums:
        copy.wait_recv()
    h1[...] = own_h0 + r1[1].astype(f32) + r1[2].astype(f32) + r1[3].astype(f32)
    norm_rows(h1, mn.at[x], mlp_gain, (0, PAD))
    rows_sent = [link.send(mn.at[x], mn.at[x], "mp", step) for step in range(1, NX)]
    gate.finish()
    up.finish()
    for copy in rows_sent:
        copy.wait_recv()
    full_mn = mn[...].reshape(4 * PAD, -1)
    for j in range(4):
        cols = pl.ds(j * 256, 256)
        wg = gb[:, :, :, :, cols].reshape(-1, 256)
        wu = ub[:, :, :, :, cols].reshape(-1, 256)
        act = jax.nn.gelu(dot(full_mn, wg), approximate=True)
        hid[:, cols] = (act * dot(full_mn, wu)).astype(bf16)
    down.finish()
    for copy in sums:
        copy.wait_send()
    full_down = flat(db)
    for j in range(4):
        value = nt(hid[...], full_down[j * 256 : (j + 1) * 256]).astype(bf16)
        part[:, :, j * 256 : (j + 1) * 256] = value.reshape(4, PAD, 256)
    sums2 = exchange(part, r2)
    own_h1 = h1[...] + part[x].astype(f32)
    for copy in sums2:
        copy.wait_recv()
    h1[...] = own_h1 + r2[1].astype(f32) + r2[2].astype(f32) + r2[3].astype(f32)
    norm_rows(h1, fn, final_gain, (0, PAD))
    velocity = nt(hdt[...], fn[...])[:, 0:span]
    vel_ref[0] = velocity
    diff = velocity - (noisev[x] - actv[x])
    square = jnp.sum(diff * diff, axis=0, keepdims=True)
    loss_ref[...] = jnp.sum(square, axis=1, keepdims=True) / (span * 32.0)
    waited = {id(copy) for copy in sums}
    for copy in link.sent:
        if id(copy) not in waited:
            copy.wait_send()


def on_device(
    prefix_hidden,
    prefix_len,
    actions,
    noise,
    time_index,
    prefix_gain,
    key_weight,
    value_weight,
    action_in,
    attn_gain,
    query_w,
    akey_w,
    avalue_w,
    out_w,
    mlp_gain,
    gate_w,
    up_w,
    down_w,
    final_gain,
    head_w,
):
    positions, width = prefix_hidden.shape[1:]
    group_eps, span, adim = actions.shape
    expert = action_in.shape[1]
    times = (time_index.astype(f32) + 0.5) / TSTEPS
    x_t = times[:, None, None] * noise + (1.0 - times)[:, None, None] * actions
    x_in = jnp.pad(x_t.astype(bf16), ((0, 0), (0, PAD - span), (0, 0)))
    x_in = x_in.reshape(group_eps * PAD, adim)
    half = expert // 2
    inv_period = (250.0 * 1000.0 ** (-np.arange(half) / (half - 1))).astype(np.float32)
    vmem = pl.BlockSpec(memory_space=pltpu.VMEM)
    smem = pl.BlockSpec(memory_space=pltpu.SMEM)
    hbm = pl.BlockSpec(memory_space=pltpu.HBM)
    operands = [
        (prefix_len, smem),
        (time_index, smem),
        (x_in, vmem),
        (actions.transpose(0, 2, 1), hbm),
        (noise.transpose(0, 2, 1), hbm),
        (prefix_hidden.reshape(positions, width), hbm),
        (jnp.asarray(inv_period)[None, :], vmem),
        (prefix_gain[None, :], vmem),
        (attn_gain[None, :], vmem),
        (mlp_gain[None, :], vmem),
        (final_gain[None, :], vmem),
        (action_in, hbm),
        (head_w.T, hbm),
        (key_weight, hbm),
        (value_weight, hbm),
        (query_w, hbm),
        (akey_w, hbm),
        (avalue_w, hbm),
        (out_w.T, hbm),
        (gate_w, hbm),
        (up_w, hbm),
        (down_w.T, hbm),
    ]

    def weight(rows, cols):
        return pltpu.VMEM((NZ, NY, NC, rows, cols), bf16)

    rows = group_eps * PAD
    velocity, loss = pl.pallas_call(
        kernel,
        out_shape=(
            jax.ShapeDtypeStruct((1, adim, span), f32),
            jax.ShapeDtypeStruct((1, 1), f32),
        ),
        in_specs=[spec for _, spec in operands],
        out_specs=(vmem, vmem),
        scratch_shapes=[
            weight(32, 256),
            weight(32, 256),
            weight(16, 512),
            weight(16, 512),
            weight(16, 512),
            weight(16, 1024),
            weight(16, 1024),
            weight(16, 1024),
            pltpu.VMEM((positions, width), bf16),
            pltpu.VMEM((positions, 256), bf16),
            pltpu.VMEM((positions, 256), bf16),
            pltpu.VMEM((adim, expert), bf16),
            pltpu.VMEM((adim, expert), bf16),
            pltpu.VMEM((group_eps, adim, span), f32),
            pltpu.VMEM((group_eps, adim, span), f32),
            pltpu.VMEM((rows, expert), f32),
            pltpu.VMEM((rows, expert), bf16),
            pltpu.VMEM((PAD, 512), bf16),
            pltpu.VMEM((NX, 2, PAD, 256), bf16),
            pltpu.VMEM((NX, 2, PAD, 256), bf16),
            pltpu.VMEM((NX, 2, PAD, 256), bf16),
            pltpu.VMEM((NX, 2, PAD, 256), bf16),
            pltpu.VMEM((NX, PAD, expert), bf16),
            pltpu.VMEM((NX, PAD, expert), bf16),
            pltpu.VMEM((NX, PAD, expert), bf16),
            pltpu.VMEM((PAD, expert), f32),
            pltpu.VMEM((NX, PAD, expert), bf16),
            pltpu.VMEM((rows, 1024), bf16),
            pltpu.VMEM((PAD, expert), bf16),
            pltpu.SemaphoreType.DMA((SENDS,)),
            pltpu.SemaphoreType.DMA((SENDS,)),
            pltpu.SemaphoreType.DMA((LOCALS,)),
        ],
        compiler_params=pltpu.CompilerParams(
            collective_id=0, has_side_effects=True, vmem_limit_bytes=56 << 20
        ),
    )(*[value for value, _ in operands])
    return velocity.transpose(0, 2, 1), loss.reshape(1)


def solution(mesh):
    split = Mesh(mesh.devices.reshape(NZ, NY, NC, NX), DP_MP)
    placed = (
        P(DP_MP, None, None),
        P(DP),
        P(DP, None, None),
        P(DP, None, None),
        P(DP),
        P(),
        P(DP, None),
        P(DP, None),
        P(),
        P(),
        P(DP, "mp"),
        P(DP, None),
        P(DP, None),
        P("mp", DP),
        P(),
        P(DP, "mp"),
        P(DP, "mp"),
        P("mp", DP),
        P(),
        P(),
    )
    return jax.shard_map(
        on_device,
        mesh=split,
        in_specs=placed,
        out_specs=(P(DP_MP, None, None), P(DP_MP)),
        check_vma=False,
    )
```

```python
import functools
import math

import jax
import jax.numpy as jnp
import numpy as np
from jax import lax
from jax.experimental import pallas as pl
from jax.experimental.pallas import tpu as pltpu
from jax.sharding import Mesh
from jax.sharding import PartitionSpec as P

TSTEPS = 1000
NZ, NY, NC, NX = 8, 4, 2, 4
SIZE = {"z": NZ, "y": NY, "c": NC, "mp": NX}
DP_MP = ("z", "y", "c", "mp")
DP = ("z", "y", "c")
MESH = pl.DeviceIdType.MESH
PAD = 64
ROWS = 56
SENDS = 192
LOCALS = 32
f32, bf16 = jnp.float32, jnp.bfloat16


def nt(a, b):
    return lax.dot_general(a, b, (((1,), (1,)), ((), ())), preferred_element_type=f32)


def dot(a, b):
    return jnp.dot(a, b, preferred_element_type=f32)


class Link:
    def __init__(self, send_sem, recv_sem):
        self.ss, self.rs = send_sem, recv_sem
        self.me = {a: lax.axis_index(a) for a in SIZE}
        self.sent = []

    def peer(self, axis, step):
        return {axis: lax.rem(self.me[axis] + step + SIZE[axis], SIZE[axis])}

    def send(self, src, dst, axis, step):
        k = len(self.sent)
        copy = pltpu.make_async_remote_copy(
            src_ref=src,
            dst_ref=dst,
            send_sem=self.ss.at[k],
            recv_sem=self.rs.at[k],
            device_id=self.peer(axis, step),
            device_id_type=MESH,
        )
        copy.start()
        self.sent.append(copy)
        return copy


class Gather:
    def __init__(self, link, buf, plan):
        self.link, self.buf = link, buf
        self.waiting = []
        self.steps = []
        for first, (dim, form) in zip((True, False), plan):
            if form == "ring":
                for hop in range(1, SIZE[dim] // 2 + 1):
                    self.steps.append(functools.partial(self.ring, dim, first, hop))
            elif form == "direct":
                self.steps.append(functools.partial(self.direct, dim, first))
            else:
                self.steps.append(functools.partial(self.two, dim, first, 1))
                self.steps.append(functools.partial(self.two, dim, first, 2))
        self.steps.append(self.core)
        self.steps.append(self.arrive)

    def at(self, dim, first, step, part=None):
        me = self.link.me
        i = lax.rem(me[dim] + step + SIZE[dim], SIZE[dim])
        cols = self.buf.shape[-1]
        half = pl.ds(0 if part is None else part * (cols // 2), cols // 2)
        if dim == "z":
            if first:
                if part is None:
                    return self.buf.at[i, me["y"], me["c"]]
                return self.buf.at[i, me["y"], me["c"], :, half]
            if part is None:
                return self.buf.at[i, :, me["c"]]
            return self.buf.at[i, pl.ds(part * (NY // 2), NY // 2), me["c"]]
        if first:
            if part is None:
                return self.buf.at[me["z"], i, me["c"]]
            return self.buf.at[me["z"], i, me["c"], :, half]
        if part is None:
            return self.buf.at[:, i, me["c"]]
        return self.buf.at[pl.ds(part * (NZ // 2), NZ // 2), i, me["c"]]

    def send(self, view, axis, step):
        self.waiting.append(self.link.send(view, view, axis, step))

    def arrive(self):
        for copy in self.waiting:
            copy.wait_recv()
        self.waiting = []

    def ring(self, dim, first, hop):
        self.arrive()
        last = hop == SIZE[dim] // 2
        self.send(self.at(dim, first, 1 - hop, 0 if last else None), dim, 1)
        self.send(self.at(dim, first, hop - 1, 1 if last else None), dim, -1)

    def direct(self, dim, first):
        self.arrive()
        for step in range(1, SIZE[dim]):
            self.send(self.at(dim, first, 0), dim, step)

    def two(self, dim, first, hop):
        self.arrive()
        if hop == 1:
            for step in (1, -1, 2, -2):
                self.send(self.at(dim, first, 0), dim, step)
        else:
            self.send(self.at(dim, first, -2), dim, 1)
            self.send(self.at(dim, first, 2), dim, -1)
            if self.buf.shape[-1] < 256:
                self.send(self.at(dim, first, -2), dim, 2)
                return
            self.send(self.at(dim, first, -2, 0), dim, 2)
            self.send(self.at(dim, first, 2, 1), dim, -2)

    def core(self):
        self.arrive()
        self.send(self.buf.at[:, :, self.link.me["c"]], "c", 1)


def flat(ref):
    return ref[...].reshape(-1, ref.shape[-1])


def norm_rows(src, dst, gain, rows, block=16, unroll=4):
    start, count = rows

    def body(i, _):
        at = pl.ds(pl.multiple_of(start + i * block, block), block)
        v = src[at, :].astype(f32)
        scale = lax.rsqrt(jnp.mean(v * v, axis=-1, keepdims=True) + 1e-06)
        dst[at, :] = (v * scale * gain[...]).astype(bf16)
        return 0

    lax.fori_loop(0, count // block, body, 0, unroll=unroll)


PLANS = {
    "k": (("z", "two"), ("y", "direct")),
    "q0": (("z", "two"), ("y", "direct")),
    "q1": (("y", "direct"), ("z", "ring")),
    "v": (("y", "direct"), ("z", "ring")),
    "a": (("z", "two"), ("y", "direct")),
    "o": (("z", "two"), ("y", "direct")),
    "g": (("z", "ring"), ("y", "ring")),
    "u": (("y", "ring"), ("z", "ring")),
    "d": (("y", "ring"), ("z", "ring")),
}
ORDER = (
    "q1.0", "k.0", "a.0", "q0.0", "v.0", "h", "q1.1", "n0", "k.1", "a.1", "v.1", "q0.1", "n1",
    "u.0", "q1.2", "g.0", "d.0", "n2", "k.2", "a.2", "o.0", "n3", "v.2", "q0.2", "u.1", "d.1",
    "q1.3", "g.1", "o.1", "v.3", "q1.4", "g.2", "o.2", "k.3", "v.4", "q1.5", "a.3", "k.4", "pk0",
    "g.3", "pk1", "q1.6", "qb", "a.4", "kv", "q0.3", "v.5", "u.2", "pk2", "d.2", "g.4", "pk3",
    "q0.4", "qa", "v.6", "pv0", "pv1", "pv2", "pv3", "t0", "u.3", "o.3", "t1", "d.3", "t2", "t3",
    "u.4", "g.5", "d.4", "o.4", "omA", "omB", "u.5", "g.6", "d.5", "mnA", "u.6", "mnB", "d.6",
    "g.7", "u.7", "fA", "d.7", "dA", "fB", "dB", "eA", "eB",
)


def kernel(
    lens,
    tix,
    acts,
    noise,
    prefix,
    inv_period,
    prefix_gain,
    attn_gain,
    mlp_gain,
    final_gain,
    action_in,
    head_t,
    key_w,
    value_w,
    query_w,
    akey_w,
    avalue_w,
    out_t,
    gate_w,
    up_w,
    down_t,
    vel_ref,
    loss_ref,
    kb,
    vb,
    q0b,
    q1b,
    ab,
    ob,
    gb,
    ub,
    db,
    pre,
    pk,
    pv,
    ain,
    hdt,
    actv,
    noisev,
    h0,
    an,
    akvs,
    akv,
    qs,
    qall,
    ares,
    aall,
    part,
    part2,
    r1,
    r2,
    h1,
    mn,
    hid,
    fn,
    send_sem,
    recv_sem,
    local_sem,
):
    link = Link(send_sem, recv_sem)
    me = link.me
    z, y, c, x = (me[a] for a in DP_MP)
    span = acts.shape[2]
    count = [0]

    def fetch(src, dst):
        copy = pltpu.make_async_copy(src, dst, local_sem.at[count[0]])
        copy.start()
        count[0] += 1
        return copy

    barrier = pltpu.get_barrier_semaphore()
    near = [("z", s) for s in (1, -1, 2, -2)] + [("y", s) for s in (1, 2, 3)]
    near += [("c", 1)] + [("mp", s) for s in (1, 2, 3)]
    for axis, step in near:
        pl.semaphore_signal(barrier, inc=1, device_id=link.peer(axis, step), device_id_type=MESH)
    side = pl.ds(pl.multiple_of(lax.rem(x, 2) * 128, 128), 128)
    quarter_sem = local_sem.at[LOCALS - 1]
    action_block = pltpu.make_async_copy(akey_w.at[:, side], ab.at[z, y, c], quarter_sem)

    @pl.when(x < 2)
    def _():
        action_block.start()

    @pl.when(x >= 2)
    def _():
        pltpu.make_async_copy(avalue_w.at[:, side], ab.at[z, y, c], quarter_sem).start()

    early = [
        action_block,
        fetch(key_w, kb.at[z, y, c]),
        fetch(query_w.at[:, pl.ds(0, 256)], q0b.at[z, y, c]),
        fetch(query_w.at[:, pl.ds(256, 256)], q1b.at[z, y, c]),
        fetch(value_w, vb.at[z, y, c]),
    ]
    small = [
        fetch(action_in, ain),
        fetch(acts, actv),
        fetch(noise, noisev),
        fetch(head_t, hdt),
    ]
    late = {
        "o": fetch(out_t, ob.at[z, y, c]),
        "g": fetch(gate_w, gb.at[z, y, c]),
        "u": fetch(up_w, ub.at[z, y, c]),
        "d": fetch(down_t, db.at[z, y, c]),
    }
    quarter = prefix.shape[0] // 4
    chunks = [
        fetch(prefix.at[pl.ds(i * quarter, quarter)], pre.at[pl.ds(i * quarter, quarter)])
        for i in range(4)
    ]
    bufs = {
        "k": kb, "v": vb, "q0": q0b, "q1": q1b, "a": ab, "o": ob, "g": gb, "u": ub, "d": db,
    }
    gathers = {name: Gather(link, buf, PLANS[name]) for name, buf in bufs.items()}
    own = pl.ds(pl.multiple_of(x * PAD, PAD), PAD)
    flight = {}
    tasks = {}

    def task(fn, name, *args):
        tasks[name] = functools.partial(fn, *args)

    def others(src, dst, rows):
        at = pl.ds(*rows)
        return [
            link.send(src.at[lax.rem(x + step, NX), at], dst.at[step, at], "mp", step)
            for step in range(1, NX)
        ]

    def arrived(name):
        for copy in flight[name]:
            copy.wait_recv()

    def embed():
        for copy in small:
            copy.wait()
        for e in range(4):
            t = (tix[e].astype(f32) + 0.5) * (1.0 / TSTEPS)
            u = t * inv_period[...]
            turn = (u - jnp.floor(u + 0.5)) * (2.0 * math.pi)
            half = turn.shape[1]
            x_t = t * noisev[e] + (1.0 - t) * actv[e]
            mixed = lax.dot_general(
                x_t.astype(bf16), ain[...], (((0,), (0,)), ((), ())), preferred_element_type=f32
            )
            h0[(e + 1) * PAD - 16 : (e + 1) * PAD, :] = jnp.zeros((16, 2 * half), f32)
            at = pl.ds(e * PAD, span)
            h0[at, 0:half] = mixed[:, 0:half] + jnp.sin(turn)
            h0[at, half:] = mixed[:, half:] + jnp.cos(turn)
        norm_rows(h0, an, attn_gain, (0, 4 * PAD))

    task(embed, "h")

    def prefix_norm(i):
        chunks[i].wait()
        norm_rows(pre, pre, prefix_gain, (i * quarter, quarter))

    def project_query(h):
        q = (dot(an[...], flat((q0b, q1b)[h])) * 0.0625).astype(bf16)
        qs[h] = q.reshape(4, PAD, 256)
        at = pl.ds(0, ROWS)
        flight["q%d" % h] = [
            link.send(qs.at[h, lax.rem(x + step, NX), at], qall.at[x, h, at], "mp", step)
            for step in range(1, NX)
        ]
        qall[x, h] = qs[h, x]

    task(project_query, "qa", 0)
    task(project_query, "qb", 1)

    def project_action():
        akvs[...] = dot(an[...], flat(ab)).astype(bf16).reshape(4, PAD, 128)
        flight["kv"] = [
            link.send(akvs.at[lax.rem(x + step, NX)], akv.at[x], "mp", step)
            for step in range(1, NX)
        ]
        akv[x] = akvs[x]

    task(project_action, "kv")

    def project_prefix(i, weight, dst):
        at = pl.ds(i * quarter, quarter)
        dst[at, :] = dot(pre[at, :], flat(weight)).astype(bf16)

    for i in range(4):
        task(prefix_norm, "n%d" % i, i)
        task(project_prefix, "pk%d" % i, i, kb, pk)
        task(project_prefix, "pv%d" % i, i, vb, pv)

    def attend(step):
        if step == 0:
            arrived("kv")
            flight["r"] = []
        src = lax.rem(x - step + NX, NX)
        if step:
            for h in range(2):
                flight["q%d" % h][step - 1].wait_recv()
        rows = qall[src].reshape(2 * PAD, 256)
        s = nt(rows, pk[...])
        live = lax.broadcasted_iota(jnp.int32, s.shape, 1) < lens[x]
        p = jnp.where(live, jnp.exp(s), 0.0)
        sa = nt(rows, jnp.concatenate([akv[0], akv[1]], axis=1))
        real = lax.broadcasted_iota(jnp.int32, sa.shape, 1) < span
        pa = jnp.where(real, jnp.exp(sa), 0.0)
        total = jnp.sum(p, axis=-1, keepdims=True) + jnp.sum(pa, axis=-1, keepdims=True)
        mixed = dot(p.astype(bf16), pv[...])
        mixed = mixed + dot(pa.astype(bf16), jnp.concatenate([akv[2], akv[3]], axis=1))
        done = (mixed / total).astype(bf16).reshape(2, PAD, 256)
        if step:
            ares[step] = done
            at = pl.ds(0, ROWS)
            flight["r"].append(
                link.send(ares.at[step, :, at], aall.at[x, :, at], "mp", -step)
            )
        else:
            aall[x] = done

    for step in range(4):
        task(attend, "t%d" % step, step)

    def out_part(wave, start, rows):
        if wave == "A":
            arrived("r")
        at = slice(start, start + 32)
        a0 = aall[:, 0, at].reshape(128, 256)
        a1 = aall[:, 1, at].reshape(128, 256)
        w = flat(ob)
        for j in range(4):
            cols = slice(j * 256, (j + 1) * 256)
            value = nt(a0, w[cols, 0:256]) + nt(a1, w[cols, 256:512])
            part[:, at, cols] = value.astype(bf16).reshape(4, 32, 256)
        flight["p" + wave] = others(part, r1, (start, rows))

    def summed(base, mine, got, at):
        return (
            base
            + mine[x, at].astype(f32)
            + got[1, at].astype(f32)
            + got[2, at].astype(f32)
            + got[3, at].astype(f32)
        )

    def middle(wave, start, rows):
        arrived("p" + wave)
        at = slice(start, start + 32)
        mine = pl.ds(pl.multiple_of(x * PAD + start, 32), 32)
        h1[at, :] = summed(h0[mine, :], part, r1, at)
        norm_rows(h1, mn.at[x], mlp_gain, (start, 32), unroll=2)
        send = pl.ds(start, rows)
        flight["m" + wave] = [
            link.send(mn.at[x, send], mn.at[x, send], "mp", step) for step in range(1, NX)
        ]

    def feed(wave, start, rows):
        arrived("m" + wave)
        rows_in = mn[:, start : start + 32].reshape(128, -1)
        at = pl.ds(start * 4, 128)
        for j in range(4):
            cols = pl.ds(j * 256, 256)
            wg = gb[:, :, :, :, cols].reshape(-1, 256)
            wu = ub[:, :, :, :, cols].reshape(-1, 256)
            act = jax.nn.gelu(dot(rows_in, wg), approximate=True)
            hid[at, cols] = (act * dot(rows_in, wu)).astype(bf16)

    def down_part(wave, start, rows):
        at = slice(start, start + 32)
        value_in = hid[start * 4 : start * 4 + 128, :]
        w = flat(db)
        for j in range(4):
            cols = slice(j * 256, (j + 1) * 256)
            value = nt(value_in, w[cols]).astype(bf16)
            part2[:, at, cols] = value.reshape(4, 32, 256)
        flight["s" + wave] = others(part2, r2, (start, rows))

    def finish(wave, start, rows):
        arrived("s" + wave)
        at = slice(start, start + 32)
        h1[at, :] = summed(h1[at, :], part2, r2, at)
        norm_rows(h1, fn, final_gain, (start, 32), unroll=2)
        if wave == "B":
            velocity = nt(hdt[...], fn[...])[:, 0:span]
            vel_ref[0] = velocity
            diff = velocity - (noisev[x] - actv[x])
            square = jnp.sum(diff * diff, axis=0, keepdims=True)
            scale = 1.0 / (diff.shape[0] * diff.shape[1])
            loss_ref[...] = jnp.sum(square, axis=1, keepdims=True) * scale

    for wave in (("A", 0, 32), ("B", 32, ROWS - 32)):
        task(out_part, "om" + wave[0], *wave)
        task(middle, "mn" + wave[0], *wave)
        task(feed, "f" + wave[0], *wave)
        task(down_part, "d" + wave[0], *wave)
        task(finish, "e" + wave[0], *wave)

    for copy in early:
        copy.wait()
    pl.semaphore_wait(barrier, len(near))
    for name in ORDER:
        if "." not in name:
            tasks[name]()
            continue
        item, step = name.split(".")
        if step == "0" and item in late:
            late[item].wait()
        gathers[item].steps[int(step)]()
    for copy in link.sent:
        copy.wait_send()


def on_device(
    prefix_hidden,
    prefix_len,
    actions,
    noise,
    time_index,
    prefix_gain,
    key_weight,
    value_weight,
    action_in,
    attn_gain,
    query_w,
    akey_w,
    avalue_w,
    out_w,
    mlp_gain,
    gate_w,
    up_w,
    down_w,
    final_gain,
    head_w,
):
    positions, width = prefix_hidden.shape[1:]
    group_eps, span, adim = actions.shape
    expert = action_in.shape[1]
    half = expert // 2
    inv_period = (250.0 * 1000.0 ** (-np.arange(half) / (half - 1))).astype(np.float32)
    vmem = pl.BlockSpec(memory_space=pltpu.VMEM)
    smem = pl.BlockSpec(memory_space=pltpu.SMEM)
    hbm = pl.BlockSpec(memory_space=pltpu.HBM)
    operands = [
        (prefix_len, smem),
        (time_index, smem),
        (actions.transpose(0, 2, 1), hbm),
        (noise.transpose(0, 2, 1), hbm),
        (prefix_hidden.reshape(positions, width), hbm),
        (jnp.asarray(inv_period)[None, :], vmem),
        (prefix_gain[None, :], vmem),
        (attn_gain[None, :], vmem),
        (mlp_gain[None, :], vmem),
        (final_gain[None, :], vmem),
        (action_in, hbm),
        (head_w.T, hbm),
        (key_weight, hbm),
        (value_weight, hbm),
        (query_w, hbm),
        (akey_w, hbm),
        (avalue_w, hbm),
        (out_w.T, hbm),
        (gate_w, hbm),
        (up_w, hbm),
        (down_w.T, hbm),
    ]

    def weight(rows, cols):
        return pltpu.VMEM((NZ, NY, NC, rows, cols), bf16)

    rows = group_eps * PAD
    velocity, loss = pl.pallas_call(
        kernel,
        out_shape=(
            jax.ShapeDtypeStruct((1, adim, span), f32),
            jax.ShapeDtypeStruct((1, 1), f32),
        ),
        in_specs=[spec for _, spec in operands],
        out_specs=(vmem, vmem),
        scratch_shapes=[
            weight(32, 256),
            weight(32, 256),
            weight(16, 256),
            weight(16, 256),
            weight(16, 128),
            weight(16, 512),
            weight(16, 1024),
            weight(16, 1024),
            weight(16, 1024),
            pltpu.VMEM((positions, width), bf16),
            pltpu.VMEM((positions, 256), bf16),
            pltpu.VMEM((positions, 256), bf16),
            pltpu.VMEM((adim, expert), bf16),
            pltpu.VMEM((adim, expert), bf16),
            pltpu.VMEM((group_eps, adim, span), f32),
            pltpu.VMEM((group_eps, adim, span), f32),
            pltpu.VMEM((rows, expert), f32),
            pltpu.VMEM((rows, expert), bf16),
            pltpu.VMEM((NX, PAD, 128), bf16),
            pltpu.VMEM((NX, PAD, 128), bf16),
            pltpu.VMEM((2, NX, PAD, 256), bf16),
            pltpu.VMEM((NX, 2, PAD, 256), bf16),
            pltpu.VMEM((NX, 2, PAD, 256), bf16),
            pltpu.VMEM((NX, 2, PAD, 256), bf16),
            pltpu.VMEM((NX, PAD, expert), bf16),
            pltpu.VMEM((NX, PAD, expert), bf16),
            pltpu.VMEM((NX, PAD, expert), bf16),
            pltpu.VMEM((NX, PAD, expert), bf16),
            pltpu.VMEM((PAD, expert), f32),
            pltpu.VMEM((NX, PAD, expert), bf16),
            pltpu.VMEM((rows, 1024), bf16),
            pltpu.VMEM((PAD, expert), bf16),
            pltpu.SemaphoreType.DMA((SENDS,)),
            pltpu.SemaphoreType.DMA((SENDS,)),
            pltpu.SemaphoreType.DMA((LOCALS,)),
        ],
        compiler_params=pltpu.CompilerParams(
            collective_id=0, has_side_effects=True, vmem_limit_bytes=56 << 20
        ),
    )(*[value for value, _ in operands])
    return velocity.transpose(0, 2, 1), loss.reshape(1)


def solution(mesh):
    split = Mesh(mesh.devices.reshape(NZ, NY, NC, NX), DP_MP)
    placed = (
        P(DP_MP, None, None),
        P(DP),
        P(DP, None, None),
        P(DP, None, None),
        P(DP),
        P(),
        P(DP, None),
        P(DP, None),
        P(),
        P(),
        P(DP, "mp"),
        P(DP, None),
        P(DP, None),
        P("mp", DP),
        P(),
        P(DP, "mp"),
        P(DP, "mp"),
        P("mp", DP),
        P(),
        P(),
    )
    return jax.shard_map(
        on_device,
        mesh=split,
        in_specs=placed,
        out_specs=(P(DP_MP, None, None), P(DP_MP)),
        check_vma=False,
    )
```

```python
import functools
import math

import jax
import jax.numpy as jnp
import numpy as np
from jax import lax
from jax.experimental import pallas as pl
from jax.experimental.pallas import tpu as pltpu
from jax.sharding import Mesh
from jax.sharding import PartitionSpec as P

TSTEPS = 1000
NZ, NY, NC, NX = 8, 4, 2, 4
SIZE = {"z": NZ, "y": NY, "c": NC, "mp": NX}
DP_MP = ("z", "y", "c", "mp")
DP = ("z", "y", "c")
MESH = pl.DeviceIdType.MESH
PAD = 64
ROWS = 56
SENDS = 192
LOCALS = 32
f32, bf16 = jnp.float32, jnp.bfloat16


def nt(a, b):
    return lax.dot_general(a, b, (((1,), (1,)), ((), ())), preferred_element_type=f32)


def dot(a, b):
    return jnp.dot(a, b, preferred_element_type=f32)


class Link:
    def __init__(self, send_sem, recv_sem):
        self.ss, self.rs = send_sem, recv_sem
        self.me = {a: lax.axis_index(a) for a in SIZE}
        self.sent = []

    def peer(self, axis, step):
        return {axis: lax.rem(self.me[axis] + step + SIZE[axis], SIZE[axis])}

    def send(self, src, dst, axis, step):
        k = len(self.sent)
        copy = pltpu.make_async_remote_copy(
            src_ref=src,
            dst_ref=dst,
            send_sem=self.ss.at[k],
            recv_sem=self.rs.at[k],
            device_id=self.peer(axis, step),
            device_id_type=MESH,
        )
        copy.start()
        self.sent.append(copy)
        return copy


class Gather:
    def __init__(self, link, buf, plan):
        self.link, self.buf = link, buf
        self.waiting = []
        self.steps = []
        for first, (dim, form) in zip((True, False), plan):
            if form == "ring":
                for hop in range(1, SIZE[dim] // 2 + 1):
                    self.steps.append(functools.partial(self.ring, dim, first, hop))
            elif form == "direct":
                self.steps.append(functools.partial(self.direct, dim, first))
            else:
                self.steps.append(functools.partial(self.two, dim, first, 1))
                self.steps.append(functools.partial(self.two, dim, first, 2))
        self.steps.append(self.core)
        self.steps.append(self.arrive)

    def at(self, dim, first, step, part=None):
        me = self.link.me
        i = lax.rem(me[dim] + step + SIZE[dim], SIZE[dim])
        cols = self.buf.shape[-1]
        half = pl.ds(0 if part is None else part * (cols // 2), cols // 2)
        if dim == "z":
            if first:
                if part is None:
                    return self.buf.at[i, me["y"], me["c"]]
                return self.buf.at[i, me["y"], me["c"], :, half]
            if part is None:
                return self.buf.at[i, :, me["c"]]
            return self.buf.at[i, pl.ds(part * (NY // 2), NY // 2), me["c"]]
        if first:
            if part is None:
                return self.buf.at[me["z"], i, me["c"]]
            return self.buf.at[me["z"], i, me["c"], :, half]
        if part is None:
            return self.buf.at[:, i, me["c"]]
        return self.buf.at[pl.ds(part * (NZ // 2), NZ // 2), i, me["c"]]

    def send(self, view, axis, step):
        self.waiting.append(self.link.send(view, view, axis, step))

    def arrive(self):
        for copy in self.waiting:
            copy.wait_recv()
        self.waiting = []

    def ring(self, dim, first, hop):
        self.arrive()
        last = hop == SIZE[dim] // 2
        self.send(self.at(dim, first, 1 - hop, 0 if last else None), dim, 1)
        self.send(self.at(dim, first, hop - 1, 1 if last else None), dim, -1)

    def direct(self, dim, first):
        self.arrive()
        for step in range(1, SIZE[dim]):
            self.send(self.at(dim, first, 0), dim, step)

    def two(self, dim, first, hop):
        self.arrive()
        if hop == 1:
            for step in (1, -1, 2, -2):
                self.send(self.at(dim, first, 0), dim, step)
        else:
            self.send(self.at(dim, first, -2), dim, 1)
            self.send(self.at(dim, first, 2), dim, -1)
            if self.buf.shape[-1] < 256:
                self.send(self.at(dim, first, -2), dim, 2)
                return
            self.send(self.at(dim, first, -2, 0), dim, 2)
            self.send(self.at(dim, first, 2, 1), dim, -2)

    def core(self):
        self.arrive()
        self.send(self.buf.at[:, :, self.link.me["c"]], "c", 1)


def flat(ref):
    return ref[...].reshape(-1, ref.shape[-1])


def norm_rows(src, dst, gain, rows, block=16, unroll=4):
    start, count = rows

    def body(i, _):
        at = pl.ds(pl.multiple_of(start + i * block, block), block)
        v = src[at, :].astype(f32)
        scale = lax.rsqrt(jnp.mean(v * v, axis=-1, keepdims=True) + 1e-06)
        dst[at, :] = (v * scale * gain[...]).astype(bf16)
        return 0

    lax.fori_loop(0, count // block, body, 0, unroll=unroll)


PLANS = {
    "k": (("z", "two"), ("y", "ring")),
    "q0": (("z", "two"), ("y", "ring")),
    "q1": (("z", "two"), ("y", "ring")),
    "v": (("y", "direct"), ("z", "ring")),
    "a": (("z", "two"), ("y", "direct")),
    "o": (("z", "ring"), ("y", "ring")),
    "g": (("z", "two"), ("y", "ring")),
    "u": (("y", "ring"), ("z", "ring")),
    "d": (("z", "two"), ("y", "ring")),
}
ORDER = (
    "q0.0", "v.0", "k.0", "o.0", "q1.0", "h", "n0", "q0.1", "v.1", "n1", "n2", "k.1", "o.1",
    "q1.1", "n3", "q0.2", "a.0", "u.0", "v.2", "k.2", "o.2", "q1.2", "g.0", "a.1", "q0.3", "u.1",
    "v.3", "o.3", "d.0", "k.3", "g.1", "a.2", "q1.3", "q0.4", "v.4", "o.4", "u.2", "q0.5", "qa",
    "k.4", "d.1", "a.3", "g.2", "q1.4", "k.5", "pk0", "v.5", "pk1", "a.4", "kv", "q1.5", "qb",
    "pk2", "pk3", "v.6", "pv0", "o.5", "u.3", "pv1", "pv2", "pv3", "t0", "d.2", "t1", "t2", "t3",
    "g.3", "u.4", "o.6", "o.7", "omA", "omB", "u.5", "d.3", "g.4", "mnA", "u.6", "mnB", "d.4",
    "g.5", "u.7", "fA", "d.5", "dA", "fB", "dB", "eA", "eB",
)


def kernel(
    lens,
    tix,
    acts,
    noise,
    prefix,
    inv_period,
    prefix_gain,
    attn_gain,
    mlp_gain,
    final_gain,
    action_in,
    head_t,
    key_w,
    value_w,
    query_w,
    akey_w,
    avalue_w,
    out_t,
    gate_w,
    up_w,
    down_t,
    vel_ref,
    loss_ref,
    kb,
    vb,
    q0b,
    q1b,
    ab,
    ob,
    gb,
    ub,
    db,
    pre,
    pk,
    pv,
    ain,
    hdt,
    actv,
    noisev,
    h0,
    an,
    akvs,
    akv,
    qs,
    qall,
    ares,
    aall,
    part,
    part2,
    r1,
    r2,
    h1,
    mn,
    hid,
    fn,
    send_sem,
    recv_sem,
    local_sem,
):
    link = Link(send_sem, recv_sem)
    me = link.me
    z, y, c, x = (me[a] for a in DP_MP)
    span = acts.shape[2]
    count = [0]

    def fetch(src, dst):
        copy = pltpu.make_async_copy(src, dst, local_sem.at[count[0]])
        copy.start()
        count[0] += 1
        return copy

    barrier = pltpu.get_barrier_semaphore()
    near = [("z", s) for s in (1, -1, 2, -2)] + [("y", s) for s in (1, 2, 3)]
    near += [("c", 1)] + [("mp", s) for s in (1, 2, 3)]
    for axis, step in near:
        pl.semaphore_signal(barrier, inc=1, device_id=link.peer(axis, step), device_id_type=MESH)
    side = pl.ds(pl.multiple_of(lax.rem(x, 2) * 128, 128), 128)
    quarter_sem = local_sem.at[LOCALS - 1]
    action_block = pltpu.make_async_copy(akey_w.at[:, side], ab.at[z, y, c], quarter_sem)

    @pl.when(x < 2)
    def _():
        action_block.start()

    @pl.when(x >= 2)
    def _():
        pltpu.make_async_copy(avalue_w.at[:, side], ab.at[z, y, c], quarter_sem).start()

    early = [
        action_block,
        fetch(key_w, kb.at[z, y, c]),
        fetch(query_w.at[:, pl.ds(0, 256)], q0b.at[z, y, c]),
        fetch(query_w.at[:, pl.ds(256, 256)], q1b.at[z, y, c]),
        fetch(value_w, vb.at[z, y, c]),
    ]
    small = [
        fetch(action_in, ain),
        fetch(acts, actv),
        fetch(noise, noisev),
        fetch(head_t, hdt),
    ]
    late = {
        "o": fetch(out_t, ob.at[z, y, c]),
        "g": fetch(gate_w, gb.at[z, y, c]),
        "u": fetch(up_w, ub.at[z, y, c]),
        "d": fetch(down_t, db.at[z, y, c]),
    }
    quarter = prefix.shape[0] // 4
    chunks = [
        fetch(prefix.at[pl.ds(i * quarter, quarter)], pre.at[pl.ds(i * quarter, quarter)])
        for i in range(4)
    ]
    bufs = {
        "k": kb, "v": vb, "q0": q0b, "q1": q1b, "a": ab, "o": ob, "g": gb, "u": ub, "d": db,
    }
    gathers = {name: Gather(link, buf, PLANS[name]) for name, buf in bufs.items()}
    own = pl.ds(pl.multiple_of(x * PAD, PAD), PAD)
    flight = {}
    tasks = {}

    def task(fn, name, *args):
        tasks[name] = functools.partial(fn, *args)

    def others(src, dst, rows):
        at = pl.ds(*rows)
        return [
            link.send(src.at[lax.rem(x + step, NX), at], dst.at[step, at], "mp", step)
            for step in range(1, NX)
        ]

    def arrived(name):
        for copy in flight[name]:
            copy.wait_recv()

    def embed():
        for copy in small:
            copy.wait()
        for e in range(4):
            t = (tix[e].astype(f32) + 0.5) * (1.0 / TSTEPS)
            u = t * inv_period[...]
            turn = (u - jnp.floor(u + 0.5)) * (2.0 * math.pi)
            half = turn.shape[1]
            x_t = t * noisev[e] + (1.0 - t) * actv[e]
            mixed = lax.dot_general(
                x_t.astype(bf16), ain[...], (((0,), (0,)), ((), ())), preferred_element_type=f32
            )
            h0[(e + 1) * PAD - 16 : (e + 1) * PAD, :] = jnp.zeros((16, 2 * half), f32)
            at = pl.ds(e * PAD, span)
            h0[at, 0:half] = mixed[:, 0:half] + jnp.sin(turn)
            h0[at, half:] = mixed[:, half:] + jnp.cos(turn)
        norm_rows(h0, an, attn_gain, (0, 4 * PAD))

    task(embed, "h")

    def prefix_norm(i):
        chunks[i].wait()
        norm_rows(pre, pre, prefix_gain, (i * quarter, quarter))

    def project_query(h):
        q = (dot(an[...], flat((q0b, q1b)[h])) * 0.0625).astype(bf16)
        qs[h] = q.reshape(4, PAD, 256)
        at = pl.ds(0, ROWS)
        flight["q%d" % h] = [
            link.send(qs.at[h, lax.rem(x + step, NX), at], qall.at[x, h, at], "mp", step)
            for step in range(1, NX)
        ]
        qall[x, h] = qs[h, x]

    task(project_query, "qa", 0)
    task(project_query, "qb", 1)

    def project_action():
        akvs[...] = dot(an[...], flat(ab)).astype(bf16).reshape(4, PAD, 128)
        flight["kv"] = [
            link.send(akvs.at[lax.rem(x + step, NX)], akv.at[x], "mp", step)
            for step in range(1, NX)
        ]
        akv[x] = akvs[x]

    task(project_action, "kv")

    def project_prefix(i, weight, dst):
        at = pl.ds(i * quarter, quarter)
        dst[at, :] = dot(pre[at, :], flat(weight)).astype(bf16)

    for i in range(4):
        task(prefix_norm, "n%d" % i, i)
        task(project_prefix, "pk%d" % i, i, kb, pk)
        task(project_prefix, "pv%d" % i, i, vb, pv)

    def attend(step):
        if step == 0:
            arrived("kv")
            flight["r"] = []
        src = lax.rem(x - step + NX, NX)
        if step:
            for h in range(2):
                flight["q%d" % h][step - 1].wait_recv()
        rows = qall[src].reshape(2 * PAD, 256)
        s = nt(rows, pk[...])
        live = lax.broadcasted_iota(jnp.int32, s.shape, 1) < lens[x]
        p = jnp.where(live, jnp.exp(s), 0.0)
        sa = nt(rows, jnp.concatenate([akv[0], akv[1]], axis=1))
        real = lax.broadcasted_iota(jnp.int32, sa.shape, 1) < span
        pa = jnp.where(real, jnp.exp(sa), 0.0)
        total = jnp.sum(p, axis=-1, keepdims=True) + jnp.sum(pa, axis=-1, keepdims=True)
        mixed = dot(p.astype(bf16), pv[...])
        mixed = mixed + dot(pa.astype(bf16), jnp.concatenate([akv[2], akv[3]], axis=1))
        done = (mixed / total).astype(bf16).reshape(2, PAD, 256)
        if step:
            ares[step] = done
            at = pl.ds(0, ROWS)
            flight["r"].append(
                link.send(ares.at[step, :, at], aall.at[x, :, at], "mp", -step)
            )
        else:
            aall[x] = done

    for step in range(4):
        task(attend, "t%d" % step, step)

    def out_part(wave, start, rows):
        if wave == "A":
            arrived("r")
        at = slice(start, start + 32)
        a0 = aall[:, 0, at].reshape(128, 256)
        a1 = aall[:, 1, at].reshape(128, 256)
        w = flat(ob)
        for j in range(4):
            cols = slice(j * 256, (j + 1) * 256)
            value = nt(a0, w[cols, 0:256]) + nt(a1, w[cols, 256:512])
            part[:, at, cols] = value.astype(bf16).reshape(4, 32, 256)
        flight["p" + wave] = others(part, r1, (start, rows))

    def summed(base, mine, got, at):
        return (
            base
            + mine[x, at].astype(f32)
            + got[1, at].astype(f32)
            + got[2, at].astype(f32)
            + got[3, at].astype(f32)
        )

    def middle(wave, start, rows):
        arrived("p" + wave)
        at = slice(start, start + 32)
        mine = pl.ds(pl.multiple_of(x * PAD + start, 32), 32)
        h1[at, :] = summed(h0[mine, :], part, r1, at)
        norm_rows(h1, mn.at[x], mlp_gain, (start, 32), unroll=2)
        send = pl.ds(start, rows)
        flight["m" + wave] = [
            link.send(mn.at[x, send], mn.at[x, send], "mp", step) for step in range(1, NX)
        ]

    def feed(wave, start, rows):
        arrived("m" + wave)
        rows_in = mn[:, start : start + 32].reshape(128, -1)
        at = pl.ds(start * 4, 128)
        for j in range(4):
            cols = pl.ds(j * 256, 256)
            wg = gb[:, :, :, :, cols].reshape(-1, 256)
            wu = ub[:, :, :, :, cols].reshape(-1, 256)
            act = jax.nn.gelu(dot(rows_in, wg), approximate=True)
            hid[at, cols] = (act * dot(rows_in, wu)).astype(bf16)

    def down_part(wave, start, rows):
        at = slice(start, start + 32)
        value_in = hid[start * 4 : start * 4 + 128, :]
        w = flat(db)
        for j in range(4):
            cols = slice(j * 256, (j + 1) * 256)
            value = nt(value_in, w[cols]).astype(bf16)
            part2[:, at, cols] = value.reshape(4, 32, 256)
        flight["s" + wave] = others(part2, r2, (start, rows))

    def finish(wave, start, rows):
        arrived("s" + wave)
        at = slice(start, start + 32)
        h1[at, :] = summed(h1[at, :], part2, r2, at)
        norm_rows(h1, fn, final_gain, (start, 32), unroll=2)
        if wave == "B":
            velocity = nt(hdt[...], fn[...])[:, 0:span]
            vel_ref[0] = velocity
            diff = velocity - (noisev[x] - actv[x])
            square = jnp.sum(diff * diff, axis=0, keepdims=True)
            scale = 1.0 / (diff.shape[0] * diff.shape[1])
            loss_ref[...] = jnp.sum(square, axis=1, keepdims=True) * scale

    for wave in (("A", 0, 32), ("B", 32, ROWS - 32)):
        task(out_part, "om" + wave[0], *wave)
        task(middle, "mn" + wave[0], *wave)
        task(feed, "f" + wave[0], *wave)
        task(down_part, "d" + wave[0], *wave)
        task(finish, "e" + wave[0], *wave)

    for copy in early:
        copy.wait()
    pl.semaphore_wait(barrier, len(near))
    for name in ORDER:
        if "." not in name:
            tasks[name]()
            continue
        item, step = name.split(".")
        if step == "0" and item in late:
            late[item].wait()
        gathers[item].steps[int(step)]()
    for copy in link.sent:
        copy.wait_send()


def on_device(
    prefix_hidden,
    prefix_len,
    actions,
    noise,
    time_index,
    prefix_gain,
    key_weight,
    value_weight,
    action_in,
    attn_gain,
    query_w,
    akey_w,
    avalue_w,
    out_w,
    mlp_gain,
    gate_w,
    up_w,
    down_w,
    final_gain,
    head_w,
):
    positions, width = prefix_hidden.shape[1:]
    group_eps, span, adim = actions.shape
    expert = action_in.shape[1]
    half = expert // 2
    inv_period = (250.0 * 1000.0 ** (-np.arange(half) / (half - 1))).astype(np.float32)
    vmem = pl.BlockSpec(memory_space=pltpu.VMEM)
    smem = pl.BlockSpec(memory_space=pltpu.SMEM)
    hbm = pl.BlockSpec(memory_space=pltpu.HBM)
    operands = [
        (prefix_len, smem),
        (time_index, smem),
        (actions.transpose(0, 2, 1), hbm),
        (noise.transpose(0, 2, 1), hbm),
        (prefix_hidden.reshape(positions, width), hbm),
        (jnp.asarray(inv_period)[None, :], vmem),
        (prefix_gain[None, :], vmem),
        (attn_gain[None, :], vmem),
        (mlp_gain[None, :], vmem),
        (final_gain[None, :], vmem),
        (action_in, hbm),
        (head_w.T, hbm),
        (key_weight, hbm),
        (value_weight, hbm),
        (query_w, hbm),
        (akey_w, hbm),
        (avalue_w, hbm),
        (out_w.T, hbm),
        (gate_w, hbm),
        (up_w, hbm),
        (down_w.T, hbm),
    ]

    def weight(rows, cols):
        return pltpu.VMEM((NZ, NY, NC, rows, cols), bf16)

    rows = group_eps * PAD
    velocity, loss = pl.pallas_call(
        kernel,
        out_shape=(
            jax.ShapeDtypeStruct((1, adim, span), f32),
            jax.ShapeDtypeStruct((1, 1), f32),
        ),
        in_specs=[spec for _, spec in operands],
        out_specs=(vmem, vmem),
        scratch_shapes=[
            weight(32, 256),
            weight(32, 256),
            weight(16, 256),
            weight(16, 256),
            weight(16, 128),
            weight(16, 512),
            weight(16, 1024),
            weight(16, 1024),
            weight(16, 1024),
            pltpu.VMEM((positions, width), bf16),
            pltpu.VMEM((positions, 256), bf16),
            pltpu.VMEM((positions, 256), bf16),
            pltpu.VMEM((adim, expert), bf16),
            pltpu.VMEM((adim, expert), bf16),
            pltpu.VMEM((group_eps, adim, span), f32),
            pltpu.VMEM((group_eps, adim, span), f32),
            pltpu.VMEM((rows, expert), f32),
            pltpu.VMEM((rows, expert), bf16),
            pltpu.VMEM((NX, PAD, 128), bf16),
            pltpu.VMEM((NX, PAD, 128), bf16),
            pltpu.VMEM((2, NX, PAD, 256), bf16),
            pltpu.VMEM((NX, 2, PAD, 256), bf16),
            pltpu.VMEM((NX, 2, PAD, 256), bf16),
            pltpu.VMEM((NX, 2, PAD, 256), bf16),
            pltpu.VMEM((NX, PAD, expert), bf16),
            pltpu.VMEM((NX, PAD, expert), bf16),
            pltpu.VMEM((NX, PAD, expert), bf16),
            pltpu.VMEM((NX, PAD, expert), bf16),
            pltpu.VMEM((PAD, expert), f32),
            pltpu.VMEM((NX, PAD, expert), bf16),
            pltpu.VMEM((rows, 1024), bf16),
            pltpu.VMEM((PAD, expert), bf16),
            pltpu.SemaphoreType.DMA((SENDS,)),
            pltpu.SemaphoreType.DMA((SENDS,)),
            pltpu.SemaphoreType.DMA((LOCALS,)),
        ],
        compiler_params=pltpu.CompilerParams(
            collective_id=0, has_side_effects=True, vmem_limit_bytes=56 << 20
        ),
    )(*[value for value, _ in operands])
    return velocity.transpose(0, 2, 1), loss.reshape(1)


def solution(mesh):
    split = Mesh(mesh.devices.reshape(NZ, NY, NC, NX), DP_MP)
    placed = (
        P(DP_MP, None, None),
        P(DP),
        P(DP, None, None),
        P(DP, None, None),
        P(DP),
        P(),
        P(DP, None),
        P(DP, None),
        P(),
        P(),
        P(DP, "mp"),
        P(DP, None),
        P(DP, None),
        P("mp", DP),
        P(),
        P(DP, "mp"),
        P(DP, "mp"),
        P("mp", DP),
        P(),
        P(),
    )
    return jax.shard_map(
        on_device,
        mesh=split,
        in_specs=placed,
        out_specs=(P(DP_MP, None, None), P(DP_MP)),
        check_vma=False,
    )
```

```python
import functools
import math

import jax
import jax.numpy as jnp
import numpy as np
from jax import lax
from jax.experimental import pallas as pl
from jax.experimental.pallas import tpu as pltpu
from jax.sharding import Mesh
from jax.sharding import PartitionSpec as P

TSTEPS = 1000
NZ, NY, NC, NX = 8, 4, 2, 4
SIZE = {"z": NZ, "y": NY, "c": NC, "mp": NX}
DP_MP = ("z", "y", "c", "mp")
DP = ("z", "y", "c")
MESH = pl.DeviceIdType.MESH
PAD = 64
ROWS = 56
SENDS = 192
LOCALS = 32
f32, bf16 = jnp.float32, jnp.bfloat16


def nt(a, b):
    return lax.dot_general(a, b, (((1,), (1,)), ((), ())), preferred_element_type=f32)


def dot(a, b):
    return jnp.dot(a, b, preferred_element_type=f32)


class Link:
    def __init__(self, send_sem, recv_sem):
        self.ss, self.rs = send_sem, recv_sem
        self.me = {a: lax.axis_index(a) for a in SIZE}
        self.sent = []

    def peer(self, axis, step):
        return {axis: lax.rem(self.me[axis] + step + SIZE[axis], SIZE[axis])}

    def send(self, src, dst, axis, step):
        k = len(self.sent)
        copy = pltpu.make_async_remote_copy(
            src_ref=src,
            dst_ref=dst,
            send_sem=self.ss.at[k],
            recv_sem=self.rs.at[k],
            device_id=self.peer(axis, step),
            device_id_type=MESH,
        )
        copy.start()
        self.sent.append(copy)
        return copy


class Gather:
    def __init__(self, link, buf, plan):
        self.link, self.buf = link, buf
        self.waiting = []
        self.steps = []
        for first, (dim, form) in zip((True, False), plan):
            if form == "ring":
                for hop in range(1, SIZE[dim] // 2 + 1):
                    self.steps.append(functools.partial(self.ring, dim, first, hop))
            elif form == "direct":
                self.steps.append(functools.partial(self.direct, dim, first))
            else:
                self.steps.append(functools.partial(self.two, dim, first, 1))
                self.steps.append(functools.partial(self.two, dim, first, 2))
        self.steps.append(self.core)
        self.steps.append(self.arrive)

    def at(self, dim, first, step, part=None):
        me = self.link.me
        i = lax.rem(me[dim] + step + SIZE[dim], SIZE[dim])
        cols = self.buf.shape[-1]
        half = pl.ds(0 if part is None else part * (cols // 2), cols // 2)
        if dim == "z":
            if first:
                if part is None:
                    return self.buf.at[i, me["y"], me["c"]]
                return self.buf.at[i, me["y"], me["c"], :, half]
            if part is None:
                return self.buf.at[i, :, me["c"]]
            return self.buf.at[i, pl.ds(part * (NY // 2), NY // 2), me["c"]]
        if first:
            if part is None:
                return self.buf.at[me["z"], i, me["c"]]
            return self.buf.at[me["z"], i, me["c"], :, half]
        if part is None:
            return self.buf.at[:, i, me["c"]]
        return self.buf.at[pl.ds(part * (NZ // 2), NZ // 2), i, me["c"]]

    def send(self, view, axis, step):
        self.waiting.append(self.link.send(view, view, axis, step))

    def arrive(self):
        for copy in self.waiting:
            copy.wait_recv()
        self.waiting = []

    def ring(self, dim, first, hop):
        self.arrive()
        last = hop == SIZE[dim] // 2
        self.send(self.at(dim, first, 1 - hop, 0 if last else None), dim, 1)
        self.send(self.at(dim, first, hop - 1, 1 if last else None), dim, -1)

    def direct(self, dim, first):
        self.arrive()
        for step in range(1, SIZE[dim]):
            self.send(self.at(dim, first, 0), dim, step)

    def two(self, dim, first, hop):
        self.arrive()
        if hop == 1:
            for step in (1, -1, 2, -2):
                self.send(self.at(dim, first, 0), dim, step)
        else:
            self.send(self.at(dim, first, -2), dim, 1)
            self.send(self.at(dim, first, 2), dim, -1)
            if self.buf.shape[-1] < 256:
                self.send(self.at(dim, first, -2), dim, 2)
                return
            self.send(self.at(dim, first, -2, 0), dim, 2)
            self.send(self.at(dim, first, 2, 1), dim, -2)

    def core(self):
        self.arrive()
        self.send(self.buf.at[:, :, self.link.me["c"]], "c", 1)


def flat(ref):
    return ref[...].reshape(-1, ref.shape[-1])


def norm_rows(src, dst, gain, rows, block=16, unroll=4):
    start, count = rows

    def body(i, _):
        at = pl.ds(pl.multiple_of(start + i * block, block), block)
        v = src[at, :].astype(f32)
        scale = lax.rsqrt(jnp.mean(v * v, axis=-1, keepdims=True) + 1e-06)
        dst[at, :] = (v * scale * gain[...]).astype(bf16)
        return 0

    lax.fori_loop(0, count // block, body, 0, unroll=unroll)


PLANS = {
    "k": (("z", "two"), ("y", "direct")),
    "q0": (("z", "two"), ("y", "direct")),
    "q1": (("y", "direct"), ("z", "ring")),
    "v": (("y", "direct"), ("z", "ring")),
    "a": (("z", "two"), ("y", "direct")),
    "o": (("z", "two"), ("y", "ring")),
    "g": (("z", "ring"), ("y", "ring")),
    "u": (("y", "ring"), ("z", "ring")),
    "d": (("y", "ring"), ("z", "ring")),
}
ORDER = (
    "q1.0", "q0.0", "v.0", "a.0", "k.0", "g.0", "q1.1", "h", "q0.1", "v.1", "a.1", "u.0", "d.0",
    "k.1", "q1.2", "g.1", "q0.2", "o.0", "v.2", "a.2", "u.1", "k.2", "q1.3", "d.1", "g.2", "n0",
    "n1", "o.1", "q0.3", "v.3", "n2", "q1.4", "a.3", "u.2", "g.3", "n3", "q0.4", "qa", "o.2",
    "a.4", "kv", "v.4", "q1.5", "q1.6", "qb", "k.3", "d.2", "u.3", "g.4", "v.5", "k.4", "pk0",
    "pk1", "pk2", "pk3", "o.3", "v.6", "pv0", "pv1", "pv2", "pv3", "t0", "t1", "d.3", "t2", "t3",
    "u.4", "g.5", "o.4", "d.4", "o.5", "omA", "omB", "u.5", "g.6", "d.5", "mnA", "u.6", "mnB",
    "d.6", "g.7", "u.7", "fA", "d.7", "dA", "fB", "dB", "eA", "eB",
)


def kernel(
    lens,
    tix,
    acts,
    noise,
    prefix,
    inv_period,
    prefix_gain,
    attn_gain,
    mlp_gain,
    final_gain,
    action_in,
    head_t,
    key_w,
    value_w,
    query_w,
    akey_w,
    avalue_w,
    out_t,
    gate_w,
    up_w,
    down_t,
    vel_ref,
    loss_ref,
    kb,
    vb,
    q0b,
    q1b,
    ab,
    ob,
    gb,
    ub,
    db,
    pre,
    pk,
    pv,
    ain,
    hdt,
    actv,
    noisev,
    h0,
    an,
    akvs,
    akv,
    qs,
    qall,
    ares,
    aall,
    part,
    part2,
    r1,
    r2,
    h1,
    mn,
    hid,
    fn,
    send_sem,
    recv_sem,
    local_sem,
):
    link = Link(send_sem, recv_sem)
    me = link.me
    z, y, c, x = (me[a] for a in DP_MP)
    span = acts.shape[2]
    count = [0]

    def fetch(src, dst):
        copy = pltpu.make_async_copy(src, dst, local_sem.at[count[0]])
        copy.start()
        count[0] += 1
        return copy

    barrier = pltpu.get_barrier_semaphore()
    near = [("z", s) for s in (1, -1, 2, -2)] + [("y", s) for s in (1, 2, 3)]
    near += [("c", 1)] + [("mp", s) for s in (1, 2, 3)]
    for axis, step in near:
        pl.semaphore_signal(barrier, inc=1, device_id=link.peer(axis, step), device_id_type=MESH)
    side = pl.ds(pl.multiple_of(lax.rem(x, 2) * 128, 128), 128)
    quarter_sem = local_sem.at[LOCALS - 1]
    action_block = pltpu.make_async_copy(akey_w.at[:, side], ab.at[z, y, c], quarter_sem)

    @pl.when(x < 2)
    def _():
        action_block.start()

    @pl.when(x >= 2)
    def _():
        pltpu.make_async_copy(avalue_w.at[:, side], ab.at[z, y, c], quarter_sem).start()

    early = [
        action_block,
        fetch(key_w, kb.at[z, y, c]),
        fetch(query_w.at[:, pl.ds(0, 256)], q0b.at[z, y, c]),
        fetch(query_w.at[:, pl.ds(256, 256)], q1b.at[z, y, c]),
        fetch(value_w, vb.at[z, y, c]),
    ]
    small = [
        fetch(action_in, ain),
        fetch(acts, actv),
        fetch(noise, noisev),
        fetch(head_t, hdt),
    ]
    late = {
        "o": fetch(out_t, ob.at[z, y, c]),
        "g": fetch(gate_w, gb.at[z, y, c]),
        "u": fetch(up_w, ub.at[z, y, c]),
        "d": fetch(down_t, db.at[z, y, c]),
    }
    quarter = prefix.shape[0] // 4
    chunks = [
        fetch(prefix.at[pl.ds(i * quarter, quarter)], pre.at[pl.ds(i * quarter, quarter)])
        for i in range(4)
    ]
    bufs = {
        "k": kb, "v": vb, "q0": q0b, "q1": q1b, "a": ab, "o": ob, "g": gb, "u": ub, "d": db,
    }
    gathers = {name: Gather(link, buf, PLANS[name]) for name, buf in bufs.items()}
    own = pl.ds(pl.multiple_of(x * PAD, PAD), PAD)
    flight = {}
    tasks = {}

    def task(fn, name, *args):
        tasks[name] = functools.partial(fn, *args)

    def others(src, dst, rows):
        at = pl.ds(*rows)
        return [
            link.send(src.at[lax.rem(x + step, NX), at], dst.at[step, at], "mp", step)
            for step in range(1, NX)
        ]

    def arrived(name):
        for copy in flight[name]:
            copy.wait_recv()

    def embed():
        for copy in small:
            copy.wait()
        for e in range(4):
            t = (tix[e].astype(f32) + 0.5) * (1.0 / TSTEPS)
            u = t * inv_period[...]
            turn = (u - jnp.floor(u + 0.5)) * (2.0 * math.pi)
            half = turn.shape[1]
            x_t = t * noisev[e] + (1.0 - t) * actv[e]
            mixed = lax.dot_general(
                x_t.astype(bf16), ain[...], (((0,), (0,)), ((), ())), preferred_element_type=f32
            )
            h0[(e + 1) * PAD - 16 : (e + 1) * PAD, :] = jnp.zeros((16, 2 * half), f32)
            at = pl.ds(e * PAD, span)
            h0[at, 0:half] = mixed[:, 0:half] + jnp.sin(turn)
            h0[at, half:] = mixed[:, half:] + jnp.cos(turn)
        norm_rows(h0, an, attn_gain, (0, 4 * PAD))

    task(embed, "h")

    def prefix_norm(i):
        chunks[i].wait()
        norm_rows(pre, pre, prefix_gain, (i * quarter, quarter))

    def project_query(h):
        q = (dot(an[...], flat((q0b, q1b)[h])) * 0.0625).astype(bf16)
        qs[h] = q.reshape(4, PAD, 256)
        at = pl.ds(0, ROWS)
        flight["q%d" % h] = [
            link.send(qs.at[h, lax.rem(x + step, NX), at], qall.at[x, h, at], "mp", step)
            for step in range(1, NX)
        ]
        qall[x, h] = qs[h, x]

    task(project_query, "qa", 0)
    task(project_query, "qb", 1)

    def project_action():
        akvs[...] = dot(an[...], flat(ab)).astype(bf16).reshape(4, PAD, 128)
        flight["kv"] = [
            link.send(akvs.at[lax.rem(x + step, NX)], akv.at[x], "mp", step)
            for step in range(1, NX)
        ]
        akv[x] = akvs[x]

    task(project_action, "kv")

    def project_prefix(i, weight, dst):
        at = pl.ds(i * quarter, quarter)
        dst[at, :] = dot(pre[at, :], flat(weight)).astype(bf16)

    for i in range(4):
        task(prefix_norm, "n%d" % i, i)
        task(project_prefix, "pk%d" % i, i, kb, pk)
        task(project_prefix, "pv%d" % i, i, vb, pv)

    def attend(step):
        if step == 0:
            arrived("kv")
            flight["r"] = []
        src = lax.rem(x - step + NX, NX)
        if step:
            for h in range(2):
                flight["q%d" % h][step - 1].wait_recv()
        rows = qall[src].reshape(2 * PAD, 256)
        s = nt(rows, pk[...])
        live = lax.broadcasted_iota(jnp.int32, s.shape, 1) < lens[x]
        p = jnp.where(live, jnp.exp(s), 0.0)
        sa = nt(rows, jnp.concatenate([akv[0], akv[1]], axis=1))
        real = lax.broadcasted_iota(jnp.int32, sa.shape, 1) < span
        pa = jnp.where(real, jnp.exp(sa), 0.0)
        total = jnp.sum(p, axis=-1, keepdims=True) + jnp.sum(pa, axis=-1, keepdims=True)
        mixed = dot(p.astype(bf16), pv[...])
        mixed = mixed + dot(pa.astype(bf16), jnp.concatenate([akv[2], akv[3]], axis=1))
        done = (mixed / total).astype(bf16).reshape(2, PAD, 256)
        if step:
            ares[step] = done
            at = pl.ds(0, ROWS)
            flight["r"].append(
                link.send(ares.at[step, :, at], aall.at[x, :, at], "mp", -step)
            )
        else:
            aall[x] = done

    for step in range(4):
        task(attend, "t%d" % step, step)

    def out_part(wave, start, rows):
        if wave == "A":
            arrived("r")
        at = slice(start, start + 32)
        a0 = aall[:, 0, at].reshape(128, 256)
        a1 = aall[:, 1, at].reshape(128, 256)
        w = flat(ob)
        for j in range(4):
            cols = slice(j * 256, (j + 1) * 256)
            value = nt(a0, w[cols, 0:256]) + nt(a1, w[cols, 256:512])
            part[:, at, cols] = value.astype(bf16).reshape(4, 32, 256)
        flight["p" + wave] = others(part, r1, (start, rows))

    def summed(base, mine, got, at):
        return (
            base
            + mine[x, at].astype(f32)
            + got[1, at].astype(f32)
            + got[2, at].astype(f32)
            + got[3, at].astype(f32)
        )

    def middle(wave, start, rows):
        arrived("p" + wave)
        at = slice(start, start + 32)
        mine = pl.ds(pl.multiple_of(x * PAD + start, 32), 32)
        h1[at, :] = summed(h0[mine, :], part, r1, at)
        norm_rows(h1, mn.at[x], mlp_gain, (start, 32), unroll=2)
        send = pl.ds(start, rows)
        flight["m" + wave] = [
            link.send(mn.at[x, send], mn.at[x, send], "mp", step) for step in range(1, NX)
        ]

    def feed(wave, start, rows):
        arrived("m" + wave)
        rows_in = mn[:, start : start + 32].reshape(128, -1)
        at = pl.ds(start * 4, 128)
        for j in range(4):
            cols = pl.ds(j * 256, 256)
            wg = gb[:, :, :, :, cols].reshape(-1, 256)
            wu = ub[:, :, :, :, cols].reshape(-1, 256)
            act = jax.nn.gelu(dot(rows_in, wg), approximate=True)
            hid[at, cols] = (act * dot(rows_in, wu)).astype(bf16)

    def down_part(wave, start, rows):
        at = slice(start, start + 32)
        value_in = hid[start * 4 : start * 4 + 128, :]
        w = flat(db)
        for j in range(4):
            cols = slice(j * 256, (j + 1) * 256)
            value = nt(value_in, w[cols]).astype(bf16)
            part2[:, at, cols] = value.reshape(4, 32, 256)
        flight["s" + wave] = others(part2, r2, (start, rows))

    def finish(wave, start, rows):
        arrived("s" + wave)
        at = slice(start, start + 32)
        h1[at, :] = summed(h1[at, :], part2, r2, at)
        norm_rows(h1, fn, final_gain, (start, 32), unroll=2)
        if wave == "B":
            velocity = nt(hdt[...], fn[...])[:, 0:span]
            vel_ref[0] = velocity
            diff = velocity - (noisev[x] - actv[x])
            square = jnp.sum(diff * diff, axis=0, keepdims=True)
            scale = 1.0 / (diff.shape[0] * diff.shape[1])
            loss_ref[...] = jnp.sum(square, axis=1, keepdims=True) * scale

    for wave in (("A", 0, 32), ("B", 32, ROWS - 32)):
        task(out_part, "om" + wave[0], *wave)
        task(middle, "mn" + wave[0], *wave)
        task(feed, "f" + wave[0], *wave)
        task(down_part, "d" + wave[0], *wave)
        task(finish, "e" + wave[0], *wave)

    for copy in early:
        copy.wait()
    pl.semaphore_wait(barrier, len(near))
    for name in ORDER:
        if "." not in name:
            tasks[name]()
            continue
        item, step = name.split(".")
        if step == "0" and item in late:
            late[item].wait()
        gathers[item].steps[int(step)]()
    for copy in link.sent:
        copy.wait_send()


def on_device(
    prefix_hidden,
    prefix_len,
    actions,
    noise,
    time_index,
    prefix_gain,
    key_weight,
    value_weight,
    action_in,
    attn_gain,
    query_w,
    akey_w,
    avalue_w,
    out_w,
    mlp_gain,
    gate_w,
    up_w,
    down_w,
    final_gain,
    head_w,
):
    positions, width = prefix_hidden.shape[1:]
    group_eps, span, adim = actions.shape
    expert = action_in.shape[1]
    half = expert // 2
    inv_period = (250.0 * 1000.0 ** (-np.arange(half) / (half - 1))).astype(np.float32)
    vmem = pl.BlockSpec(memory_space=pltpu.VMEM)
    smem = pl.BlockSpec(memory_space=pltpu.SMEM)
    hbm = pl.BlockSpec(memory_space=pltpu.HBM)
    operands = [
        (prefix_len, smem),
        (time_index, smem),
        (actions.transpose(0, 2, 1), hbm),
        (noise.transpose(0, 2, 1), hbm),
        (prefix_hidden.reshape(positions, width), hbm),
        (jnp.asarray(inv_period)[None, :], vmem),
        (prefix_gain[None, :], vmem),
        (attn_gain[None, :], vmem),
        (mlp_gain[None, :], vmem),
        (final_gain[None, :], vmem),
        (action_in, hbm),
        (head_w.T, hbm),
        (key_weight, hbm),
        (value_weight, hbm),
        (query_w, hbm),
        (akey_w, hbm),
        (avalue_w, hbm),
        (out_w.T, hbm),
        (gate_w, hbm),
        (up_w, hbm),
        (down_w.T, hbm),
    ]

    def weight(rows, cols):
        return pltpu.VMEM((NZ, NY, NC, rows, cols), bf16)

    rows = group_eps * PAD
    velocity, loss = pl.pallas_call(
        kernel,
        out_shape=(
            jax.ShapeDtypeStruct((1, adim, span), f32),
            jax.ShapeDtypeStruct((1, 1), f32),
        ),
        in_specs=[spec for _, spec in operands],
        out_specs=(vmem, vmem),
        scratch_shapes=[
            weight(32, 256),
            weight(32, 256),
            weight(16, 256),
            weight(16, 256),
            weight(16, 128),
            weight(16, 512),
            weight(16, 1024),
            weight(16, 1024),
            weight(16, 1024),
            pltpu.VMEM((positions, width), bf16),
            pltpu.VMEM((positions, 256), bf16),
            pltpu.VMEM((positions, 256), bf16),
            pltpu.VMEM((adim, expert), bf16),
            pltpu.VMEM((adim, expert), bf16),
            pltpu.VMEM((group_eps, adim, span), f32),
            pltpu.VMEM((group_eps, adim, span), f32),
            pltpu.VMEM((rows, expert), f32),
            pltpu.VMEM((rows, expert), bf16),
            pltpu.VMEM((NX, PAD, 128), bf16),
            pltpu.VMEM((NX, PAD, 128), bf16),
            pltpu.VMEM((2, NX, PAD, 256), bf16),
            pltpu.VMEM((NX, 2, PAD, 256), bf16),
            pltpu.VMEM((NX, 2, PAD, 256), bf16),
            pltpu.VMEM((NX, 2, PAD, 256), bf16),
            pltpu.VMEM((NX, PAD, expert), bf16),
            pltpu.VMEM((NX, PAD, expert), bf16),
            pltpu.VMEM((NX, PAD, expert), bf16),
            pltpu.VMEM((NX, PAD, expert), bf16),
            pltpu.VMEM((PAD, expert), f32),
            pltpu.VMEM((NX, PAD, expert), bf16),
            pltpu.VMEM((rows, 1024), bf16),
            pltpu.VMEM((PAD, expert), bf16),
            pltpu.SemaphoreType.DMA((SENDS,)),
            pltpu.SemaphoreType.DMA((SENDS,)),
            pltpu.SemaphoreType.DMA((LOCALS,)),
        ],
        compiler_params=pltpu.CompilerParams(
            collective_id=0, has_side_effects=True, vmem_limit_bytes=56 << 20
        ),
    )(*[value for value, _ in operands])
    return velocity.transpose(0, 2, 1), loss.reshape(1)


def solution(mesh):
    split = Mesh(mesh.devices.reshape(NZ, NY, NC, NX), DP_MP)
    placed = (
        P(DP_MP, None, None),
        P(DP),
        P(DP, None, None),
        P(DP, None, None),
        P(DP),
        P(),
        P(DP, None),
        P(DP, None),
        P(),
        P(),
        P(DP, "mp"),
        P(DP, None),
        P(DP, None),
        P("mp", DP),
        P(),
        P(DP, "mp"),
        P(DP, "mp"),
        P("mp", DP),
        P(),
        P(),
    )
    return jax.shard_map(
        on_device,
        mesh=split,
        in_specs=placed,
        out_specs=(P(DP_MP, None, None), P(DP_MP)),
        check_vma=False,
    )
```
